256 devices in a mesh: lat: 32 (over y_hi, z, core), lon: 8 (over x, y_lo).
Axes of the slice: x: 4, y: 4 (y_hi: 2, y_lo: 2; y = y_hi * 2 + y_lo), z: 8, core: 2. Of those that a mesh axis runs over, the one named last changes fastest.
Arguments:
- inputs: bfloat16 [2048, 512, 128], P('lat', 'lon'), may hold values from -6 to 6
- w_first: bfloat16 [221184], P(('lat', 'lon')), may hold values from -0.1875 to 0.1875
- w_second: bfloat16 [331776], P(('lat', 'lon')), may hold values from -0.15625 to 0.15625
- w_third: bfloat16 [331776], P(('lat', 'lon')), may hold values from -0.15625 to 0.15625
- cotangent: bfloat16 [1024, 256, 192], P('lat', 'lon'), may hold values from -6 to 6
Outputs:
- features: bfloat16 [1024, 256, 192], P('lat', 'lon')
- grad_input: bfloat16 [2048, 512, 128], P('lat', 'lon')
- grad_first: float32 [221184], P(('lat', 'lon'))
- grad_second: float32 [331776], P(('lat', 'lon'))
- grad_third: float32 [331776], P(('lat', 'lon'))
The draws below stay inside these ranges and needn't reach their ends.
All inputs are finite; a program needn't handle non-finite values.
Results may differ from the reference program's by a relative error of at most 0.011.
Values may be sent and summed in bfloat16 or wider, within the bound.
A program may use at most 64 MiB of HBM per device.

```python
import jax
import jax.numpy as jnp
from jax import lax

C0 = 128
C1 = 192
H = 2048
W = 512
LOSS_CELLS = 1024
WS1 = 221184
WS2 = 331776


def steps_of(rng, dims, cuts, least, largest):
    factor_of = 1.0
    for axis_at, blocks in cuts:
        heights = jax.random.uniform(jax.random.fold_in(jax.random.fold_in(rng, 6), axis_at), (blocks,), jnp.float32, least / len(cuts), largest / len(cuts))
        factor_of = factor_of * jnp.repeat(jnp.exp(heights), dims[axis_at] // blocks).reshape((-1,) + (1,) * (len(dims) - 1 - axis_at))
    return factor_of


def noise(own_key, shape, width, most, shards=(), dtype=jnp.bfloat16):
    array = width * jax.random.normal(own_key, shape, jnp.float32)
    if shards:
        array = array * steps_of(own_key, shape, shards, -0.22, 0.18)
    return jnp.clip(array, -most, most).astype(dtype)


def setup_inputs(seed: int = 0) -> dict:
    seeds = jax.random.split(jax.random.key(seed), 6)
    return {
        "inputs": noise(seeds[0], (H, W, C0), 1.0, 6.0, ((0, 32), (1, 8))),
        "w_first": noise(seeds[1], (WS1,), (9 * C0) ** -0.5, 0.1875, ((0, 256),)),
        "w_second": noise(seeds[2], (WS2,), (9 * C1) ** -0.5, 0.15625, ((0, 256),)),
        "w_third": noise(seeds[3], (WS2,), (9 * C1) ** -0.5, 0.15625, ((0, 256),)),
        "cotangent": noise(seeds[4], (H // 2, W // 2, C1), 1.0, 6.0, ((0, 32), (1, 8))),
    }


LAYOUT = ('NHWC', 'HWIO', 'NHWC')

def convolve(values, kernel, stride, padding, dilation):
    result = lax.conv_general_dilated(values[None].astype(jnp.float32), kernel.astype(jnp.float32), (stride, stride), padding, lhs_dilation=(dilation, dilation), dimension_numbers=LAYOUT, precision=lax.Precision.HIGHEST)
    return result[0]

def surround(values):
    wrapped = jnp.concatenate([values[:, -1:], values, values[:, :1]], axis=1)
    return jnp.pad(wrapped, ((1, 1), (0, 0), (0, 0)))

def flipped(kernel):
    return jnp.transpose(kernel[::-1, ::-1], (0, 1, 3, 2))

def derivative(preact):
    logistic = jax.nn.sigmoid(preact)
    return logistic * (1.0 + preact * (1.0 - logistic))

def kernel_grad(padded, deltas, stride):
    row_count, col_count = (deltas.shape[0], deltas.shape[1])
    tap_terms = []
    for row_tap in range(3):
        for col_tap in range(3):
            window = padded[row_tap:row_tap + stride * (row_count - 1) + 1:stride, col_tap:col_tap + stride * (col_count - 1) + 1:stride]
            tap_terms.append(jnp.einsum('hwc,hwo->co', window.astype(jnp.float32), deltas.astype(jnp.float32), precision=lax.Precision.HIGHEST))
    return jnp.stack(tap_terms).reshape(-1) / LOSS_CELLS

def reference(inputs, w_first, w_second, w_third, cotangent):
    kernel_one = w_first.reshape(3, 3, C0, C1)
    kernel_two = w_second.reshape(3, 3, C1, C1)
    kernel_three = w_third.reshape(3, 3, C1, C1)
    flat_pad = ((0, 0), (0, 0))
    padded_in = jnp.pad(jnp.concatenate([inputs[:, -1:], inputs], axis=1), ((1, 0), (0, 0), (0, 0)))
    h_one = convolve(padded_in, kernel_one, 2, flat_pad, 1).astype(jnp.bfloat16)
    padded_one = surround(h_one)
    pre_two = convolve(padded_one, kernel_two, 1, flat_pad, 1)
    h_two = jax.nn.silu(pre_two).astype(jnp.bfloat16)
    padded_two = surround(h_two)
    pre_three = convolve(padded_two, kernel_three, 1, flat_pad, 1)
    features = jax.nn.silu(pre_three).astype(jnp.bfloat16)
    delta_three = (cotangent.astype(jnp.float32) * derivative(pre_three)).astype(jnp.bfloat16)
    grad_third = kernel_grad(padded_two, delta_three, 1)
    back_two = convolve(surround(delta_three), flipped(kernel_three), 1, flat_pad, 1)
    delta_two = (back_two * derivative(pre_two)).astype(jnp.bfloat16)
    grad_second = kernel_grad(padded_one, delta_two, 1)
    back_one = convolve(surround(delta_two), flipped(kernel_two), 1, flat_pad, 1).astype(jnp.bfloat16)
    grad_first = kernel_grad(padded_in, back_one, 2)
    extended = jnp.concatenate([back_one, back_one[:, :1]], axis=1)
    extended = jnp.pad(extended, ((0, 1), (0, 0), (0, 0)))
    grad_input = convolve(extended, flipped(kernel_one), 1, ((1, 0), (1, 0)), 2).astype(jnp.bfloat16)
    return (features, grad_input, grad_first, grad_second, grad_third)
```

```python
import functools
import jax, jax.numpy as jnp
from jax import lax
from jax.experimental import pallas as pl
from jax.experimental.pallas import tpu as pltpu
from jax.sharding import PartitionSpec as P

LOSS_CELLS = 1024
F32, BF16 = jnp.float32, jnp.bfloat16
W = 48
def mm(a, b):
    return lax.dot_general(a, b, (((1,), (0,)), ((), ())), preferred_element_type=F32)
def mmt(a, b):
    return lax.dot_general(a, b, (((1,), (1,)), ((), ())), preferred_element_type=F32)

def compute_kernel(lat_ref, x_ref, xe_ref, xw_ref, xn_ref, xs_ref, c_ref, ce_ref, cw_ref, cn_ref, cs_ref, w_ref,
                   feat_ref, gin_ref, gb_ref,
                   xf, x0, x1, kf, k1, k2, k3, cf, hs1, hs2, ds3, ds2, bs, p2, dt, g1, g23, st, of, il):
    lat = lat_ref[0]
    last = lat_ref[1]
    for g in range(32):
        v = w_ref[g].astype(F32)
        kf[54 * g : 54 * g + 54, :] = v[0:54]
        of[36 * g : 36 * g + 18, :] = v[54:72, 0:192]
        of[36 * g + 18 : 36 * g + 36, :] = v[54:72, 192:384]
    k1[...] = of[0:1152, :].astype(BF16)
    k2[...] = kf[:, 0:192].astype(BF16)
    k3[...] = kf[:, 192:384].astype(BF16)
    north = (lat > 0).astype(F32)
    south = (lat < last).astype(F32)

    def put_row(p, own, east, west, scale):
        slot = lax.rem(p, 2)
        row = xf.at[slot]
        own, east, west = own.astype(F32) * scale, east.astype(F32) * scale, west.astype(F32) * scale
        row[8:72, :] = own
        row[72:88, :] = east
        row[88:104, :] = west
        row[0:8, :] = west[8:16]
    def split_row(slot, dst, idx):
        row = xf.at[slot]
        dst[idx, :, 0:128] = row[pl.ds(7, W, stride=2), :].astype(BF16)
        dst[idx, :, 128:256] = row[pl.ds(8, W, stride=2), :].astype(BF16)
        dst[idx, :, 256:384] = row[pl.ds(9, W, stride=2), :].astype(BF16)
    def own_rows(k, _):
        r = 2 * k
        for d in range(2):
            slot = (9 + d) % 2
            put_row(slot, x_ref[r + d], xe_ref[r + d], xw_ref[r + d], 1.0)
        split_row(1, x1, k + 4)
        split_row(0, x0, k + 5)
        return 0
    lax.fori_loop(0, 32, own_rows, 0)
    for q in range(1, 10):
        p = q - 1
        put_row(p % 2, xn_ref[q, 0:64], xn_ref[q, 64:80], xn_ref[q, 80:96], north)
        split_row(p % 2, x0 if p % 2 == 0 else x1, p // 2)
    for q in range(10):
        p = 73 + q
        put_row(p % 2, xs_ref[q, 0:64], xs_ref[q, 64:80], xs_ref[q, 80:96], south)
        split_row(p % 2, x0 if p % 2 == 0 else x1, p // 2)

    def cot(idx, row, east, west):
        cf[idx, 0:32, :] = row.astype(F32)
        cf[idx, 32:40, :] = east[0:8].astype(F32)
        cf[idx, 40:48, :] = west[8:16].astype(F32)
    def cot_own(k, _):
        cot(k + 2, c_ref[k], ce_ref[k].astype(F32), cw_ref[k].astype(F32))
        return 0
    lax.fori_loop(0, 32, cot_own, 0)
    for q in range(2):
        v = cn_ref[q + 1].astype(F32)
        cot(q, v[0:32], v[32:48], v[48:64])
    for q in range(3):
        v = cs_ref[q].astype(F32)
        cot(q + 34, v[0:32], v[32:48], v[48:64])

    def rows_ok(start, n, first):
        i = lax.broadcasted_iota(jnp.int32, (n, W, 192), 0) + (start + first)
        glob = i + 32 * lat
        return (glob >= 0) & (glob < 32 * (last + 1))
    def put_shifted(dst, start, n, value):
        dst[1, pl.ds(start, n)] = value.astype(BF16)
        dst[0, pl.ds(start, n)] = pltpu.roll(value, 1, 1).astype(BF16)
        dst[2, pl.ds(start, n)] = pltpu.roll(value, W - 1, 1).astype(BF16)
    def chunks(total, n, body):
        count = -(-total // n)
        def step(k, _):
            body(jnp.minimum(k * n, total - n))
            return 0
        lax.fori_loop(0, count, step, 0)

    def h_one(s):
        n = 14
        acc = mm(x0[pl.ds(s, n)].reshape(n * W, 384), k1[0:384])
        acc += mm(x1[pl.ds(s, n)].reshape(n * W, 384), k1[384:768])
        acc += mm(x0[pl.ds(s + 1, n)].reshape(n * W, 384), k1[768:1152])
        v = jnp.where(rows_ok(s, n, -4), acc.reshape(n, W, 192), 0.0)
        put_shifted(hs1, s, n, v)
    chunks(41, 14, h_one)

    def conv(src, k, s, n):
        acc = None
        for a in range(3):
            for b in range(3):
                t = mm(src[b, pl.ds(s + a, n)].reshape(n * W, 192), k[(3 * a + b) * 192 : (3 * a + b + 1) * 192])
                acc = t if acc is None else acc + t
        return acc.reshape(n, W, 192)
    def tconv(src, k, s, n):
        acc = None
        for a in range(3):
            for b in range(3):
                t = mmt(src[2 - b, pl.ds(s + 2 - a, n)].reshape(n * W, 192), k[(3 * a + b) * 192 : (3 * a + b + 1) * 192])
                acc = t if acc is None else acc + t
        return acc.reshape(n, W, 192)

    def h_two(s):
        n = 13
        v = conv(hs1, k2, s, n)
        p2[pl.ds(s, n)] = v
        h = v / (1.0 + jnp.exp(-v))
        put_shifted(hs2, s, n, jnp.where(rows_ok(s, n, -3), h, 0.0))
    chunks(39, 13, h_two)

    def deriv(v):
        sg = 1.0 / (1.0 + jnp.exp(-v))
        return sg, sg * (1.0 + v * (1.0 - sg))
    ft = bs
    def d_three(s):
        n = 13
        v = conv(hs2, k3, s, n)
        sg, dv = deriv(v)
        ft[1, pl.ds(s, n)] = (v * sg).astype(BF16)
        d = jnp.where(rows_ok(s, n, -2), cf[pl.ds(s, n)] * dv, 0.0)
        put_shifted(ds3, s, n, d)
    chunks(37, 13, d_three)
    feat_ref[...] = ft[1, 2:34, 0:32, :]

    def wgrad(src, off, dst, lo):
        for a in range(3):
            for b in range(3):
                win = src[b, off + a : off + a + 32, 0:32, :].reshape(1024, 192)
                t = mm(dt[...], win)
                n0 = (3 * a + b) * 192
                dst[n0 : n0 + 192, lo : lo + 192] = t.T
    dt[...] = ds3[1, 2:34, 0:32, :].reshape(1024, 192).T
    wgrad(hs2, 2, g23, 192)

    def d_two(s):
        n = 12
        v = tconv(ds3, k3, s, n)
        _, dv = deriv(p2[pl.ds(s + 2, n)])
        d = jnp.where(rows_ok(s, n, -1), v * dv, 0.0)
        put_shifted(ds2, s, n, d)
    chunks(35, 12, d_two)
    dt[...] = ds2[1, 1:33, 0:32, :].reshape(1024, 192).T
    wgrad(hs1, 3, g23, 0)

    def b_one(s):
        n = 11
        v = tconv(ds2, k2, s, n)
        v = jnp.where(rows_ok(s, n, 0), v, 0.0)
        bs[1, pl.ds(s, n)] = v.astype(BF16)
        bs[2, pl.ds(s, n)] = pltpu.roll(v, W - 1, 1).astype(BF16)
    chunks(33, 11, b_one)
    dt[...] = bs[1, 0:32, 0:32, :].reshape(1024, 192).T
    for a in range(3):
        src = x1 if a == 1 else x0
        off = 4 + (a == 2)
        win = src[off : off + 32, 0:32, :].reshape(1024, 384)
        t = mm(dt[...], win)
        g1[384 * a : 384 * a + 384, :] = t.T

    for g in range(32):
        st[0:54, :] = g23[54 * g : 54 * g + 54, :]
        st[54:72, 0:192] = g1[36 * g : 36 * g + 18, :]
        st[54:72, 192:384] = g1[36 * g + 18 : 36 * g + 36, :]
        gb_ref[g] = st[...].astype(BF16)

    def k1t(a, b):
        n0 = (3 * a + b) * 128
        return k1[n0 : n0 + 128]
    def gin(s):
        n = 8
        i = s
        here = bs[1, pl.ds(i, n), 0:32, :].reshape(n * 32, 192)
        right = bs[2, pl.ds(i, n), 0:32, :].reshape(n * 32, 192)
        below = bs[1, pl.ds(i + 1, n), 0:32, :].reshape(n * 32, 192)
        corner = bs[2, pl.ds(i + 1, n), 0:32, :].reshape(n * 32, 192)
        ee = mmt(here, k1t(1, 1))
        eo = mmt(right, k1t(1, 0)) + mmt(here, k1t(1, 2))
        oe = mmt(below, k1t(0, 1)) + mmt(here, k1t(2, 1))
        oo = mmt(corner, k1t(0, 0)) + mmt(below, k1t(0, 2)) + mmt(right, k1t(2, 0)) + mmt(here, k1t(2, 2))
        il[pl.ds(0, n * 32, stride=2), :] = ee
        il[pl.ds(1, n * 32, stride=2), :] = eo
        il[pl.ds(n * 64, n * 32, stride=2), :] = oe
        il[pl.ds(n * 64 + 1, n * 32, stride=2), :] = oo
        even = il[0 : n * 64, :].reshape(n, 64, 128).astype(BF16)
        odd = il[n * 64 : n * 128, :].reshape(n, 64, 128).astype(BF16)
        for m in range(n):
            gin_ref[2 * (i + m)] = even[m]
            gin_ref[2 * (i + m) + 1] = odd[m]
    chunks(32, 8, gin)

def compute(lat2, x, xe, xw, xn, xs, c, ce, cw, cn, cs, w):
    V = pltpu.VMEM
    vm = pl.BlockSpec(memory_space=pltpu.VMEM)
    return pl.pallas_call(
        compute_kernel,
        out_shape=(jax.ShapeDtypeStruct((32, 32, 192), BF16), jax.ShapeDtypeStruct((64, 64, 128), BF16),
                   jax.ShapeDtypeStruct((32, 72, 384), BF16)),
        in_specs=[pl.BlockSpec(memory_space=pltpu.SMEM)] + [vm] * 11,
        out_specs=(vm, vm, vm),
        scratch_shapes=[
            V((2, 104, 128), F32), V((42, W, 384), BF16), V((42, W, 384), BF16),
            V((1728, 384), F32), V((1152, 192), BF16), V((1728, 192), BF16), V((1728, 192), BF16),
            V((37, W, 192), F32), V((3, 41, W, 192), BF16), V((3, 39, W, 192), BF16),
            V((3, 37, W, 192), BF16), V((3, 35, W, 192), BF16), V((3, 37, W, 192), BF16),
            V((39, W, 192), F32), V((192, 1024), BF16), V((1152, 192), F32), V((1728, 384), F32), V((72, 384), F32),
            V((1152, 192), F32), V((1024, 128), F32),
        ],
        compiler_params=pltpu.CompilerParams(vmem_limit_bytes=60 * 1024 * 1024),
        cost_estimate=pl.CostEstimate(flops=8_000_000_000, bytes_accessed=8_000_000, transcendentals=0),
        name="level_compute",
    )(lat2, x, xe, xw, xn, xs, c, ce, cw, cn, cs, w)


MESH = pl.DeviceIdType.MESH
LON, ZS, GROUPS = 8, 8, 32
S1, S2 = 864, 1296


def pieces(size, base_row, base_lane, per_row):
    out = []
    total = size * LON
    for row in range(total // 192):
        at = row * 192
        while at < (row + 1) * 192:
            shard = at // size
            end = min((row + 1) * 192, (shard + 1) * size)
            lane = at - row * 192
            out.append((shard, at - shard * size, row, lane, end - at))
            at = end
    return out


def group_map():
    moves = []
    for shard, lane, row, at, n in pieces(S1, 0, 0, 0):
        moves.append((shard, lane, 54 + row % 18, 192 * (row // 18) + at, n))
    for k in range(2):
        for shard, lane, row, at, n in pieces(S2, 0, 0, 0):
            moves.append((shard, S1 + k * S2 + lane, row, 192 * k + at, n))
    return moves


def place():
    lat, lon = lax.axis_index("lat"), lax.axis_index("lon")
    core = lax.rem(lat, 2)
    z = lax.rem(lax.div(lat, 2), ZS)
    yh = lax.div(lat, 2 * ZS)
    return lat, lon, yh, z, core


def barrier(peers):
    sem = pltpu.get_barrier_semaphore()
    for peer in peers:
        pl.semaphore_signal(sem, inc=1, device_id=peer, device_id_type=MESH)
    pl.semaphore_wait(sem, len(peers))


def gather_kernel(v_ref, x_ref, c_ref, xe, xw, xn, xs, ce, cw, cn, cs, wb,
                  vbuf, stage, own, vsend, vrecv, hsend, hrecv, wsend, wrecv, osem):
    lat, lon, yh, z, core = place()
    east, west = lax.rem(lon + 1, LON), lax.rem(lon + LON - 1, LON)
    north, south = lax.rem(lat + 31, 32), lax.rem(lat + 1, 32)
    partner = lat + 1 - 2 * core
    across = lax.rem(lat + 16, 32)
    def at_z(k):
        return yh * 16 + lax.rem(z + k + ZS, ZS) * 2 + core
    lons = [lax.rem(lon + d, LON) for d in range(1, LON)]
    barrier([(lat, p) for p in lons] + [(q, lon) for q in (north, south, across, at_z(1), at_z(-1))])

    def remote(src, dst, send, recv, peer):
        return pltpu.make_async_remote_copy(src_ref=src, dst_ref=dst, send_sem=send, recv_sem=recv,
                                            device_id=peer, device_id_type=MESH)
    vs = []
    for d in range(1, LON):
        k = remote(v_ref, vbuf.at[lon], vsend.at[d], vrecv.at[lon], (lat, lons[d - 1]))
        k.start()
        vs.append(k)
    halos = []
    def halo(src, dst, peer):
        n = len(halos)
        k = remote(src, dst, hsend.at[n], hrecv.at[n], peer)
        k.start()
        halos.append(k)
    e, w, n, s = (lat, east), (lat, west), (north, lon), (south, lon)
    halo(x_ref.at[:, 0:16], xe, w)
    halo(x_ref.at[:, 48:64], xw, e)
    halo(c_ref.at[:, 0:16], ce, w)
    halo(c_ref.at[:, 16:32], cw, e)
    halo(x_ref.at[54:64], xn.at[:, 0:64], s)
    halo(x_ref.at[0:10], xs.at[:, 0:64], n)
    halo(c_ref.at[29:32], cn.at[:, 0:32], s)
    halo(c_ref.at[0:3], cs.at[:, 0:32], n)

    vbuf[lon] = v_ref[...]
    for d in range(1, LON):
        src = lons[d - 1]
        remote(v_ref, vbuf.at[src], vsend.at[d], vrecv.at[src], (lat, src)).wait_recv()
    for shard, lane, row, at, length in group_map():
        stage[row : row + 1, at : at + length] = vbuf[shard, :, lane : lane + length]
    own[...] = stage[...].astype(BF16)

    started = []
    def send(src, slot, peer):
        k = remote(src, wb.at[slot], wsend.at[len(started)], wrecv.at[slot], peer)
        k.start()
        started.append(k)
    def arrived(slot):
        remote(own, wb.at[slot], wsend.at[0], wrecv.at[slot], (partner, lon)).wait_recv()
    up, down = (at_z(1), lon), (at_z(-1), lon)
    mine = pltpu.make_async_copy(own, wb.at[lat], osem)
    mine.start()
    send(own, lat, up)
    send(own, lat, down)
    send(own, lat, (across, lon))
    send(own, lat, (partner, lon))

    for k in range(4):
        halos[k].wait_recv()
    halo(xe.at[54:64], xn.at[:, 64:80], s)
    halo(xw.at[54:64], xn.at[:, 80:96], s)
    halo(xe.at[0:10], xs.at[:, 64:80], n)
    halo(xw.at[0:10], xs.at[:, 80:96], n)
    halo(ce.at[29:32], cn.at[:, 32:48], s)
    halo(cw.at[29:32], cn.at[:, 48:64], s)
    halo(ce.at[0:3], cs.at[:, 32:48], n)
    halo(cw.at[0:3], cs.at[:, 48:64], n)

    def slot_of(half, k):
        return half * 16 + lax.rem(z + k + ZS, ZS) * 2 + core
    other = 1 - yh
    second = slot_of(other, 0)
    def pass_on(half, t, sign, last):
        slot = slot_of(half, -sign * t)
        arrived(slot)
        if t < last:
            send(wb.at[slot], slot, up if sign > 0 else down)
        send(wb.at[slot], slot, (partner, lon))
    for t in range(0, 5):
        if t >= 1:
            if t <= 4:
                pass_on(yh, t, 1, 4)
            if t <= 3:
                pass_on(yh, t, -1, 3)
        if t == 0:
            arrived(second)
            send(wb.at[second], second, up)
            send(wb.at[second], second, down)
            send(wb.at[second], second, (partner, lon))
        else:
            if t <= 3:
                pass_on(other, t, 1, 3)
            if t <= 4:
                pass_on(other, t, -1, 4)
    for half in range(2):
        for k in range(ZS):
            arrived(half * 16 + k * 2 + 1 - core)
    mine.wait()
    for k in started:
        k.wait_send()
    for k in vs:
        k.wait_send()
    for n, k in enumerate(halos):
        k.wait_send()
        if n >= 4:
            k.wait_recv()


def gather(v, x, c):
    anyspec = pl.BlockSpec(memory_space=pl.ANY)
    sds = jax.ShapeDtypeStruct
    return pl.pallas_call(
        gather_kernel,
        out_shape=(sds((64, 16, 128), BF16), sds((64, 16, 128), BF16), sds((10, 96, 128), BF16), sds((10, 96, 128), BF16),
                   sds((32, 16, 192), BF16), sds((32, 16, 192), BF16), sds((3, 64, 192), BF16), sds((3, 64, 192), BF16),
                   sds((32, 72, 384), BF16)),
        in_specs=[pl.BlockSpec(memory_space=pltpu.VMEM), anyspec, anyspec],
        out_specs=(anyspec,) * 9,
        scratch_shapes=[
            pltpu.VMEM((LON, 1, 3456), F32), pltpu.VMEM((72, 384), F32), pltpu.VMEM((72, 384), BF16),
            pltpu.SemaphoreType.DMA((LON,)), pltpu.SemaphoreType.DMA((LON,)),
            pltpu.SemaphoreType.DMA((16,)), pltpu.SemaphoreType.DMA((16,)),
            pltpu.SemaphoreType.DMA((34,)), pltpu.SemaphoreType.DMA((GROUPS,)), pltpu.SemaphoreType.DMA,
        ],
        compiler_params=pltpu.CompilerParams(collective_id=0, has_side_effects=True),
        name="gather_weights",
    )(v, x, c)


def reduce_kernel(gb, o1, o2, o3, r1, sbuf, r2, acc, own3, r3, blk, pbuf, r4,
                  a_send, a_recv, z_send, z_recv, y_sem, l_send, l_recv):
    lat, lon, yh, z, core = place()
    partner = lat + 1 - 2 * core
    across = lax.rem(lat + 16, 32)
    lons = [lax.rem(lon + d, LON) for d in range(1, LON)]
    zs = [lax.rem(z + d, ZS) for d in range(ZS)]
    def lat_of(zz):
        return yh * 16 + zz * 2 + core
    barrier([(lat, p) for p in lons] + [(partner, lon), (across, lon)] + [(lat_of(zz), lon) for zz in zs[1:]])

    def remote(src, dst, send, recv, peer):
        return pltpu.make_async_remote_copy(src_ref=src, dst_ref=dst, send_sem=send, recv_sem=recv,
                                            device_id=peer, device_id_type=MESH)
    order = (4, 3, 5, 2, 6, 1, 7, 0)
    first = []
    for d in order:
        zz = zs[d]
        k = remote(gb.at[:, zz, 1 - core], r1.at[zz], a_send.at[zz], a_recv.at[zz], (partner, lon))
        k.start()
        first.append(k)
    sent = []
    for d, k in zip(order, first):
        zz = zs[d]
        k.wait_recv()
        total = gb[:, zz, core].astype(F32) + r1[zz].astype(F32)
        if d:
            sbuf[d] = total.astype(BF16)
            m = remote(sbuf.at[d], r2.at[z], z_send.at[d], z_recv.at[z], (lat_of(zz), lon))
            m.start()
            sent.append(m)
        else:
            acc[...] = total
    for d in (1, 7, 2, 6, 3, 5, 4):
        zz = zs[d]
        remote(sbuf.at[d], r2.at[zz], z_send.at[d], z_recv.at[zz], (lat_of(zz), lon)).wait_recv()
        acc[...] += r2[zz].astype(F32)
    own3[...] = acc[1 - yh].astype(BF16)
    y = remote(own3, r3, y_sem.at[0], y_sem.at[1], (across, lon))
    y.start()
    y.wait_recv()
    blk[...] = acc[yh] + r3[...].astype(F32)
    for shard, lane, row, at, length in group_map():
        pbuf[shard, :, lane : lane + length] = blk[row : row + 1, at : at + length]
    out = []
    for d in range(1, LON):
        p = lons[d - 1]
        k = remote(pbuf.at[p], r4.at[lon], l_send.at[d], l_recv.at[lon], (lat, p))
        k.start()
        out.append(k)
    r4[lon] = pbuf[lon]
    for d in range(1, LON):
        p = lons[d - 1]
        remote(pbuf.at[p], r4.at[p], l_send.at[d], l_recv.at[p], (lat, p)).wait_recv()
    total = r4[0]
    for n in range(1, LON):
        total = total + r4[n]
    total = total * (1.0 / LOSS_CELLS)
    o1[...] = total[:, 0:S1]
    o2[...] = total[:, S1 : S1 + S2]
    o3[...] = total[:, S1 + S2 :]
    for k in first + sent + [y] + out:
        k.wait_send()


def reduce_grads(gb):
    vm = pl.BlockSpec(memory_space=pltpu.VMEM)
    sds = jax.ShapeDtypeStruct
    V, D = pltpu.VMEM, pltpu.SemaphoreType.DMA
    return pl.pallas_call(
        reduce_kernel,
        out_shape=(sds((1, S1), F32), sds((1, S2), F32), sds((1, S2), F32)),
        in_specs=[vm],
        out_specs=(vm, vm, vm),
        scratch_shapes=[
            V((ZS, 2, 72, 384), BF16), V((ZS, 2, 72, 384), BF16), V((ZS, 2, 72, 384), BF16), V((2, 72, 384), F32),
            V((72, 384), BF16), V((72, 384), BF16), V((72, 384), F32), V((LON, 1, 3456), F32), V((LON, 1, 3456), F32),
            D((ZS,)), D((ZS,)), D((ZS,)), D((ZS,)), D((2,)), D((LON,)), D((LON,)),
        ],
        compiler_params=pltpu.CompilerParams(collective_id=1, has_side_effects=True),
        name="reduce_grads",
    )(gb)


def local(inputs, w_first, w_second, w_third, cotangent):
    v = jnp.concatenate([w_first, w_second, w_third]).astype(F32).reshape(1, -1)
    xe, xw, xn, xs, ce, cw, cn, cs, wb = gather(v, inputs, cotangent)
    where = jnp.stack([lax.axis_index("lat"), jnp.int32(lax.axis_size("lat") - 1)]).astype(jnp.int32)
    features, grad_input, gb = compute(where, inputs, xe, xw, xn, xs, cotangent, ce, cw, cn, cs, wb)
    g1, g2, g3 = reduce_grads(gb.reshape(2, ZS, 2, 72, 384))
    return features, grad_input, g1.reshape(-1), g2.reshape(-1), g3.reshape(-1)


def solution(mesh):
    tile, flat = P("lat", "lon", None), P(("lat", "lon"))
    return jax.shard_map(
        local,
        mesh=mesh,
        in_specs=(tile, flat, flat, flat, tile),
        out_specs=(tile, tile, flat, flat, flat),
        check_vma=False,
    )
```

```python
import jax
import jax.numpy as jnp
from jax import lax
from jax.experimental import pallas as pl
from jax.experimental.pallas import tpu as pltpu
from jax.sharding import PartitionSpec as P

LOSS_CELLS = 1024
F32, BF16 = jnp.float32, jnp.bfloat16
W = 48
PITCH = 104
MESH = pl.DeviceIdType.MESH
LON, ZS, GROUPS = 8, 8, 32
S1, S2 = 864, 1296


def mm(a, b):
    return lax.dot_general(a, b, (((1,), (0,)), ((), ())), preferred_element_type=F32)


def mmt(a, b):
    return lax.dot_general(a, b, (((1,), (1,)), ((), ())), preferred_element_type=F32)


def pieces(size, fold):
    out = []
    for row in range(size * LON // 192):
        at = row * 192
        while at < (row + 1) * 192:
            shard = at // size
            end = min((row + 1) * 192, (shard + 1) * size)
            out.append((shard, at - shard * size, row % fold, 192 * (row // fold) + at - row * 192, end - at))
            at = end
    return out


def group_map():
    moves = [(s, lane, 54 + row, at, n) for s, lane, row, at, n in pieces(S1, 18)]
    for k in range(2):
        moves += [(s, S1 + k * S2 + lane, row, 192 * k + at, n) for s, lane, row, at, n in pieces(S2, 54)]
    return moves


def place():
    lat, lon = lax.axis_index("lat"), lax.axis_index("lon")
    core = lax.rem(lat, 2)
    z = lax.rem(lax.div(lat, 2), ZS)
    yh = lax.div(lat, 2 * ZS)
    return lat, lon, yh, z, core


def barrier(peers):
    sem = pltpu.get_barrier_semaphore()
    for peer in peers:
        pl.semaphore_signal(sem, inc=1, device_id=peer, device_id_type=MESH)
    pl.semaphore_wait(sem, len(peers))


def remote(src, dst, send, recv, peer):
    return pltpu.make_async_remote_copy(src_ref=src, dst_ref=dst, send_sem=send, recv_sem=recv,
                                        device_id=peer, device_id_type=MESH)


def gather_kernel(w1, w2, w3, x_ref, c_ref,
                  xe, xw, xn, xs, xne, xnw, xse, xsw, ce, cw, cn, cs, cne, cnw, cse, csw, wb,
                  v_ref, vbuf, stage, own, xin, col, eb, vsend, vrecv, hsend, hrecv, wsend, wrecv, osem, isem):
    lat, lon, yh, z, core = place()
    east, west = lax.rem(lon + 1, LON), lax.rem(lon + LON - 1, LON)
    north, south = lax.rem(lat + 31, 32), lax.rem(lat + 1, 32)
    partner = lat + 1 - 2 * core
    across = lax.rem(lat + 16, 32)
    def at_z(k):
        return yh * 16 + lax.rem(z + k + ZS, ZS) * 2 + core
    lons = [lax.rem(lon + d, LON) for d in range(1, LON)]

    edges = [pltpu.make_async_copy(x_ref.at[:, 16 * (3 * k) : 16 * (3 * k) + 16], xin.at[k], isem.at[k]) for k in range(2)]
    for k in edges:
        k.start()
    v_ref[0:1, 0:S1] = w1[...].astype(F32).reshape(1, S1)
    v_ref[0:1, S1 : S1 + S2] = w2[...].astype(F32).reshape(1, S2)
    v_ref[0:1, S1 + S2 :] = w3[...].astype(F32).reshape(1, S2)
    barrier([(lat, p) for p in lons] + [(q, lon) for q in (north, south, across, at_z(1), at_z(-1))])

    vs = []
    for d in range(1, LON):
        k = remote(v_ref, vbuf.at[lon], vsend.at[d], vrecv.at[lon], (lat, lons[d - 1]))
        k.start()
        vs.append(k)
    halos = []
    def halo(src, dst, peer):
        n = len(halos)
        k = remote(src, dst, hsend.at[n], hrecv.at[n], peer)
        k.start()
        halos.append(k)
    e, w, n, s = (lat, east), (lat, west), (north, lon), (south, lon)
    for k in range(2):
        edges[k].wait()
        col[...] = xin[k].astype(F32).reshape(1024, 128)
        for j in range(10):
            eb[k, j] = col[pl.ds(j + 6 * k, 64, stride=16), :].astype(BF16)
    halo(eb.at[0], xe, w)
    halo(eb.at[1], xw, e)
    halo(x_ref.at[54:64], xn, s)
    halo(x_ref.at[0:10], xs, n)

    vbuf[lon] = v_ref[...]
    for d in range(1, LON):
        src = lons[d - 1]
        remote(v_ref, vbuf.at[src], vsend.at[d], vrecv.at[src], (lat, src)).wait_recv()
    for shard, lane, row, at, length in group_map():
        stage[row : row + 1, at : at + length] = vbuf[shard, :, lane : lane + length]
    own[...] = stage[...].astype(BF16)

    started = []
    def send(src, slot, peer):
        k = remote(src, wb.at[slot], wsend.at[len(started)], wrecv.at[slot], peer)
        k.start()
        started.append(k)
    def arrived(slot):
        remote(own, wb.at[slot], wsend.at[0], wrecv.at[slot], (partner, lon)).wait_recv()
    up, down = (at_z(1), lon), (at_z(-1), lon)
    mine = pltpu.make_async_copy(own, wb.at[lat], osem)
    mine.start()
    send(own, lat, (across, lon))
    send(own, lat, up)
    send(own, lat, down)
    send(own, lat, (partner, lon))
    halo(c_ref.at[:, 0:8], ce, w)
    halo(c_ref.at[:, 24:32], cw, e)
    halo(c_ref.at[29:32], cn, s)
    halo(c_ref.at[0:3], cs, n)

    def slot_of(half, k):
        return half * 16 + lax.rem(z + k + ZS, ZS) * 2 + core
    other = 1 - yh
    second = slot_of(other, 0)
    def pass_on(half, t, sign, last):
        slot = slot_of(half, -sign * t)
        arrived(slot)
        if t < last:
            send(wb.at[slot], slot, up if sign > 0 else down)
        send(wb.at[slot], slot, (partner, lon))
    for t in range(0, 5):
        if t >= 1:
            if t <= 4:
                pass_on(yh, t, 1, 4)
            if t <= 3:
                pass_on(yh, t, -1, 3)
        if t == 0:
            arrived(second)
            send(wb.at[second], second, up)
            send(wb.at[second], second, down)
            send(wb.at[second], second, (partner, lon))
        else:
            if t <= 3:
                pass_on(other, t, 1, 3)
            if t <= 4:
                pass_on(other, t, -1, 4)
        if t == 2:
            halos[0].wait_recv()
            halos[1].wait_recv()
            halo(xe.at[:, 48:64], xne, s)
            halo(xw.at[:, 48:64], xnw, s)
            halo(xe.at[:, 0:16], xse, n)
            halo(xw.at[:, 0:16], xsw, n)
        if t == 3:
            halos[4].wait_recv()
            halos[5].wait_recv()
            halo(ce.at[29:32], cne, s)
            halo(cw.at[29:32], cnw, s)
            halo(ce.at[0:3], cse, n)
            halo(cw.at[0:3], csw, n)
    for half in range(2):
        for k in range(ZS):
            arrived(half * 16 + k * 2 + 1 - core)
    mine.wait()
    for k in started:
        k.wait_send()
    for k in vs:
        k.wait_send()
    for n, k in enumerate(halos):
        k.wait_send()
        if n not in (0, 1, 4, 5):
            k.wait_recv()


def gather(w1, w2, w3, x, c):
    anyspec = pl.BlockSpec(memory_space=pl.ANY)
    vm = pl.BlockSpec(memory_space=pltpu.VMEM)
    shapes = ([(10, 64, 128)] * 4 + [(10, 16, 128)] * 4 + [(32, 8, 192)] * 2 + [(3, 32, 192)] * 2 + [(3, 8, 192)] * 4
              + [(32, 72, 384)])
    D = pltpu.SemaphoreType.DMA
    return pl.pallas_call(
        gather_kernel,
        out_shape=tuple(jax.ShapeDtypeStruct(s, BF16) for s in shapes),
        in_specs=[vm, vm, vm, anyspec, anyspec],
        out_specs=(anyspec,) * len(shapes),
        scratch_shapes=[
            pltpu.VMEM((1, 3456), F32), pltpu.VMEM((LON, 1, 3456), F32), pltpu.VMEM((72, 384), F32),
            pltpu.VMEM((72, 384), BF16), pltpu.VMEM((2, 64, 16, 128), BF16), pltpu.VMEM((1024, 128), F32),
            pltpu.VMEM((2, 10, 64, 128), BF16),
            D((LON,)), D((LON,)), D((16,)), D((16,)), D((34,)), D((GROUPS,)), D, D((2,)),
        ],
        compiler_params=pltpu.CompilerParams(collective_id=0, has_side_effects=True),
        name="gather_weights",
    )(w1, w2, w3, x, c)


def level_kernel(x_ref, xe, xw, xn, xs, xne, xnw, xse, xsw, c_ref, ce, cw, cn, cs, cne, cnw, cse, csw, w_ref,
                 feat_ref, gin_ref, o1, o2, o3,
                 xf, x0, x1, kf, kg, k1, k2, k3, cf, hs1, hs2, ds3, ds2, bs, p2, dt, g1, g2, g3, st, il,
                 a3, a2, a1, r3, r2, r1, s3, s2, s1, z3, z2, z1, acc3, acc2, acc1, y3s, y2s, y1s, y3, y2, y1,
                 blk, p23, p1, l23, l1, a_send, a_recv, z_send, z_recv, y_send, y_recv, l_send, l_recv):
    lat, lon, yh, z, core = place()
    last = lax.axis_size("lat") - 1
    partner = lat + 1 - 2 * core
    across = lax.rem(lat + 16, 32)
    lons = [lax.rem(lon + d, LON) for d in range(1, LON)]
    zs = [lax.rem(z + d, ZS) for d in range(ZS)]
    def lat_of(zz):
        return yh * 16 + zz * 2 + core
    barrier([(lat, p) for p in lons] + [(partner, lon), (across, lon)] + [(lat_of(zz), lon) for zz in zs[1:]])

    for g in range(32):
        v = w_ref[g].astype(F32)
        kf[54 * g : 54 * g + 54, :] = v[0:54]
        kg[36 * g : 36 * g + 18, :] = v[54:72, 0:192]
        kg[36 * g + 18 : 36 * g + 36, :] = v[54:72, 192:384]
    k1[...] = kg[...].astype(BF16)
    k2[...] = kf[:, 0:192].astype(BF16)
    k3[...] = kf[:, 192:384].astype(BF16)
    north = (lat > 0).astype(F32)
    south = (lat < last).astype(F32)

    def own_row(r, _):
        p = pl.multiple_of((r + 9) * PITCH, 8)
        xf[pl.ds(p + 8, 64), :] = x_ref[r].astype(F32)
        xf[pl.ds(p + 80, 16), :] = jnp.zeros((16, 128), F32)
        return 0
    lax.fori_loop(0, 64, own_row, 0)
    for q in range(9):
        xf[q * PITCH + 8 : q * PITCH + 72, :] = xn[q + 1].astype(F32) * north
        xf[q * PITCH + 80 : q * PITCH + 96, :] = jnp.zeros((16, 128), F32)
    for q in range(10):
        xf[(q + 73) * PITCH + 8 : (q + 73) * PITCH + 72, :] = xs[q].astype(F32) * south
        xf[(q + 73) * PITCH + 80 : (q + 73) * PITCH + 96, :] = jnp.zeros((16, 128), F32)
    for j in range(10):
        for ref, rn, rs, ats in ((xe, xne, xse, (72 + j,)), (xw, xnw, xsw, (94 + j, j - 2))):
            mid = ref[j].astype(F32)
            top = rn[j].astype(F32)[7:16] * north
            low = rs[j].astype(F32)[0:10] * south
            for at in ats:
                if at >= 0:
                    xf[pl.ds(9 * PITCH + at, 64, stride=PITCH), :] = mid
                    xf[pl.ds(at, 9, stride=PITCH), :] = top
                    xf[pl.ds(73 * PITCH + at, 10, stride=PITCH), :] = low
    def split(dst, p, idx):
        for k in range(3):
            dst[idx, :, 128 * k : 128 * k + 128] = xf[pl.ds(p * PITCH + 7 + k, W, stride=2), :].astype(BF16)
    def split_pair(k, _):
        split(x0, 2 * k, k)
        split(x1, 2 * k + 1, k)
        return 0
    lax.fori_loop(0, 41, split_pair, 0)
    split(x0, 82, 41)

    def cot(idx, row, e, w):
        cf[idx, 0:32, :] = row.astype(F32)
        cf[idx, 32:40, :] = e.astype(F32)
        cf[idx, 40:48, :] = w.astype(F32)
    def cot_own(k, _):
        cot(k + 2, c_ref[k], ce[k], cw[k])
        return 0
    lax.fori_loop(0, 32, cot_own, 0)
    for q in range(2):
        cot(q, cn[q + 1], cne[q + 1], cnw[q + 1])
    for q in range(3):
        cot(q + 34, cs[q], cse[q], csw[q])

    def rows_ok(start, n, first):
        i = lax.broadcasted_iota(jnp.int32, (n, W, 192), 0) + (start + first)
        glob = i + 32 * lat
        return (glob >= 0) & (glob < 32 * (last + 1))
    def put_shifted(dst, start, n, value):
        dst[1, pl.ds(start, n)] = value.astype(BF16)
        dst[0, pl.ds(start, n)] = pltpu.roll(value, 1, 1).astype(BF16)
        dst[2, pl.ds(start, n)] = pltpu.roll(value, W - 1, 1).astype(BF16)
    def chunks(total, n, body, lo=0, hi=None):
        count = -(-total // n)
        def step(k, _):
            body(jnp.minimum(k * n, total - n))
            return 0
        lax.fori_loop(lo, count if hi is None else hi, step, 0)

    def h_one(s):
        n = 14
        acc = mm(x0[pl.ds(s, n)].reshape(n * W, 384), k1[0:384])
        acc += mm(x1[pl.ds(s, n)].reshape(n * W, 384), k1[384:768])
        acc += mm(x0[pl.ds(s + 1, n)].reshape(n * W, 384), k1[768:1152])
        put_shifted(hs1, s, n, jnp.where(rows_ok(s, n, -4), acc.reshape(n, W, 192), 0.0))
    chunks(41, 14, h_one)

    def conv(src, k, s, n):
        acc = None
        for a in range(3):
            for b in range(3):
                t = mm(src[b, pl.ds(s + a, n)].reshape(n * W, 192), k[(3 * a + b) * 192 : (3 * a + b + 1) * 192])
                acc = t if acc is None else acc + t
        return acc.reshape(n, W, 192)
    def tconv(src, k, s, n):
        acc = None
        for a in range(3):
            for b in range(3):
                t = mmt(src[2 - b, pl.ds(s + 2 - a, n)].reshape(n * W, 192), k[(3 * a + b) * 192 : (3 * a + b + 1) * 192])
                acc = t if acc is None else acc + t
        return acc.reshape(n, W, 192)

    def h_two(s):
        n = 13
        v = conv(hs1, k2, s, n)
        p2[pl.ds(s, n)] = v
        h = v / (1.0 + jnp.exp(-v))
        put_shifted(hs2, s, n, jnp.where(rows_ok(s, n, -3), h, 0.0))
    chunks(39, 13, h_two)

    def deriv(v):
        sg = 1.0 / (1.0 + jnp.exp(-v))
        return sg, sg * (1.0 + v * (1.0 - sg))
    def d_three(s):
        n = 13
        v = conv(hs2, k3, s, n)
        sg, dv = deriv(v)
        bs[1, pl.ds(s, n)] = (v * sg).astype(BF16)
        put_shifted(ds3, s, n, jnp.where(rows_ok(s, n, -2), cf[pl.ds(s, n)] * dv, 0.0))
    chunks(37, 13, d_three)
    feat_ref[...] = bs[1, 2:34, 0:32, :]

    def wgrad(src, off, dst):
        for a in range(3):
            for b in range(3):
                win = src[b, off + a : off + a + 32, 0:32, :].reshape(1024, 192)
                t = mm(dt[...], win)
                n0 = (3 * a + b) * 192
                dst[n0 : n0 + 192, :] = t.T
    sends = []
    def to_partner(i, g, half, a, r):
        for zz in range(ZS):
            for c in range(2):
                for y in range(2):
                    base = (y * 16 + zz * 2 + c) * 2 * half
                    st[y * half : (y + 1) * half, 0:192] = g[base : base + half, :]
                    st[y * half : (y + 1) * half, 192:384] = g[base + half : base + 2 * half, :]
                a[zz, c] = st[0 : 2 * half, :].astype(BF16)
        k = remote(a.at[:, 1 - core], r, a_send.at[i], a_recv.at[i], (partner, lon))
        k.start()
        sends.append(k)
        return k
    def along_z(i, k, a, r, s, zb, acc):
        k.wait_recv()
        for d in (4, 3, 5, 2, 6, 1, 7, 0):
            zz = zs[d]
            total = a[zz, core].astype(F32) + r[zz].astype(F32)
            if d:
                s[d] = total.astype(BF16)
                m = remote(s.at[d], zb.at[z], z_send.at[i, d], z_recv.at[i, z], (lat_of(zz), lon))
                m.start()
                sends.append(m)
            else:
                acc[...] = total
    def sum_z(i, s, zb, acc, half, ys, yr):
        for d in (1, 7, 2, 6, 3, 5, 4):
            zz = zs[d]
            remote(s.at[d], zb.at[zz], z_send.at[i, d], z_recv.at[i, zz], (lat_of(zz), lon)).wait_recv()
            acc[...] += zb[zz].astype(F32)
        ys[...] = jnp.where(yh == 0, acc[half : 2 * half], acc[0:half]).astype(BF16)
        m = remote(ys, yr, y_send.at[i], y_recv.at[i], (across, lon))
        m.start()
        sends.append(m)
        return m
    def sum_y(m, acc, half, yr):
        m.wait_recv()
        blk[0:half, :] = jnp.where(yh == 0, acc[0:half], acc[half : 2 * half]) + yr[...].astype(F32)
    def to_lon(i, pb, lb):
        for d in range(1, LON):
            p = lons[d - 1]
            k = remote(pb.at[p], lb.at[lon], l_send.at[i, d], l_recv.at[i, lon], (lat, p))
            k.start()
            sends.append(k)
        lb[lon] = pb[lon]
    def sum_lon(i, pb, lb):
        for d in range(1, LON):
            p = lons[d - 1]
            remote(pb.at[p], lb.at[p], l_send.at[i, d], l_recv.at[i, p], (lat, p)).wait_recv()
        total = lb[0]
        for n in range(1, LON):
            total = total + lb[n]
        return total * (1.0 / LOSS_CELLS)

    dt[...] = ds3[1, 2:34, 0:32, :].reshape(1024, 192).T
    wgrad(hs2, 2, g3)
    c3 = to_partner(0, g3, 27, a3, r3)

    def d_two(s):
        n = 12
        v = tconv(ds3, k3, s, n)
        _, dv = deriv(p2[pl.ds(s + 2, n)])
        put_shifted(ds2, s, n, jnp.where(rows_ok(s, n, -1), v * dv, 0.0))
    chunks(35, 12, d_two)
    along_z(0, c3, a3, r3, s3, z3, acc3)
    dt[...] = ds2[1, 1:33, 0:32, :].reshape(1024, 192).T
    wgrad(hs1, 3, g2)
    c2 = to_partner(1, g2, 27, a2, r2)

    def b_one(s):
        n = 11
        v = jnp.where(rows_ok(s, n, 0), tconv(ds2, k2, s, n), 0.0)
        bs[1, pl.ds(s, n)] = v.astype(BF16)
        bs[2, pl.ds(s, n)] = pltpu.roll(v, W - 1, 1).astype(BF16)
    chunks(33, 11, b_one)
    along_z(1, c2, a2, r2, s2, z2, acc2)
    dt[...] = bs[1, 0:32, 0:32, :].reshape(1024, 192).T
    for a in range(3):
        src = x1 if a == 1 else x0
        off = 4 + (a == 2)
        win = src[off : off + 32, 0:32, :].reshape(1024, 384)
        g1[384 * a : 384 * a + 384, :] = mm(dt[...], win).T
    c1 = to_partner(2, g1, 18, a1, r1)

    def k1t(a, b):
        n0 = (3 * a + b) * 128
        return k1[n0 : n0 + 128]
    def gin(i):
        n = 8
        here = bs[1, pl.ds(i, n), 0:32, :].reshape(n * 32, 192)
        right = bs[2, pl.ds(i, n), 0:32, :].reshape(n * 32, 192)
        below = bs[1, pl.ds(i + 1, n), 0:32, :].reshape(n * 32, 192)
        corner = bs[2, pl.ds(i + 1, n), 0:32, :].reshape(n * 32, 192)
        ee = mmt(here, k1t(1, 1))
        eo = mmt(right, k1t(1, 0)) + mmt(here, k1t(1, 2))
        oe = mmt(below, k1t(0, 1)) + mmt(here, k1t(2, 1))
        oo = mmt(corner, k1t(0, 0)) + mmt(below, k1t(0, 2)) + mmt(right, k1t(2, 0)) + mmt(here, k1t(2, 2))
        il[pl.ds(0, n * 32, stride=2), :] = ee
        il[pl.ds(1, n * 32, stride=2), :] = eo
        il[pl.ds(n * 64, n * 32, stride=2), :] = oe
        il[pl.ds(n * 64 + 1, n * 32, stride=2), :] = oo
        even = il[0 : n * 64, :].reshape(n, 64, 128).astype(BF16)
        odd = il[n * 64 : n * 128, :].reshape(n, 64, 128).astype(BF16)
        for m in range(n):
            gin_ref[2 * (i + m)] = even[m]
            gin_ref[2 * (i + m) + 1] = odd[m]
    chunks(32, 8, gin, 0, 1)
    along_z(2, c1, a1, r1, s1, z1, acc1)
    chunks(32, 8, gin, 1, 4)

    m3 = sum_z(0, s3, z3, acc3, 27, y3s, y3)
    m2 = sum_z(1, s2, z2, acc2, 27, y2s, y2)
    sum_y(m3, acc3, 27, y3)
    for shard, lane, row, at, length in pieces(S2, 27):
        p23[shard, :, S2 + lane : S2 + lane + length] = blk[row : row + 1, at : at + length]
    sum_y(m2, acc2, 27, y2)
    for shard, lane, row, at, length in pieces(S2, 27):
        p23[shard, :, lane : lane + length] = blk[row : row + 1, at : at + length]
    to_lon(0, p23, l23)
    m1 = sum_z(2, s1, z1, acc1, 18, y1s, y1)
    total = sum_lon(0, p23, l23)
    o2[...] = total[:, 0:S2].reshape(S2)
    o3[...] = total[:, S2:].reshape(S2)
    sum_y(m1, acc1, 18, y1)
    for shard, lane, row, at, length in pieces(S1, 18):
        p1[shard, :, lane : lane + length] = blk[row : row + 1, at : at + length]
    to_lon(1, p1, l1)
    o1[...] = sum_lon(1, p1, l1).reshape(S1)
    for k in sends:
        k.wait_send()


def level(x, c, halos):
    V, D = pltpu.VMEM, pltpu.SemaphoreType.DMA
    vm = pl.BlockSpec(memory_space=pltpu.VMEM)
    sds = jax.ShapeDtypeStruct
    args = (x, *halos[0:8], c, *halos[8:17])
    def over_rows(*shape_of):
        return [V(shape_of[0](rows), shape_of[1]) for rows in (54, 54, 36)]
    return pl.pallas_call(
        level_kernel,
        out_shape=(sds((32, 32, 192), BF16), sds((64, 64, 128), BF16), sds((S1,), F32), sds((S2,), F32), sds((S2,), F32)),
        in_specs=[vm] * len(args),
        out_specs=(vm,) * 5,
        scratch_shapes=[
            V((83 * PITCH, 128), F32), V((42, W, 384), BF16), V((42, W, 384), BF16),
            V((1728, 384), F32), V((1152, 192), F32), V((1152, 192), BF16), V((1728, 192), BF16), V((1728, 192), BF16),
            V((37, W, 192), F32), V((3, 41, W, 192), BF16), V((3, 39, W, 192), BF16),
            V((3, 37, W, 192), BF16), V((3, 35, W, 192), BF16), V((3, 37, W, 192), BF16),
            V((39, W, 192), F32), V((192, 1024), BF16), V((1152, 192), F32), V((1728, 192), F32), V((1728, 192), F32),
            V((54, 384), F32), V((1024, 128), F32),
            *over_rows(lambda r: (ZS, 2, r, 384), BF16),
            *over_rows(lambda r: (ZS, r, 384), BF16),
            *over_rows(lambda r: (ZS, r, 384), BF16),
            *over_rows(lambda r: (ZS, r, 384), BF16),
            *over_rows(lambda r: (r, 384), F32),
            *over_rows(lambda r: (r // 2, 384), BF16),
            *over_rows(lambda r: (r // 2, 384), BF16),
            V((27, 384), F32), V((LON, 1, 2 * S2), F32), V((LON, 1, S1), F32), V((LON, 1, 2 * S2), F32), V((LON, 1, S1), F32),
            D((3,)), D((3,)), D((3, ZS)), D((3, ZS)), D((3,)), D((3,)), D((2, LON)), D((2, LON)),
        ],
        compiler_params=pltpu.CompilerParams(collective_id=1, has_side_effects=True, vmem_limit_bytes=62 * 1024 * 1024),
        name="level",
    )(*args)


def local(inputs, w_first, w_second, w_third, cotangent):
    halos = gather(w_first, w_second, w_third, inputs, cotangent)
    return level(inputs, cotangent, halos)


def solution(mesh):
    tile, flat = P("lat", "lon", None), P(("lat", "lon"))
    return jax.shard_map(
        local,
        mesh=mesh,
        in_specs=(tile, flat, flat, flat, tile),
        out_specs=(tile, tile, flat, flat, flat),
        check_vma=False,
    )
```

```python
import jax
import jax.numpy as jnp
from jax import lax
from jax.experimental import pallas as pl
from jax.experimental.pallas import tpu as pltpu
from jax.sharding import PartitionSpec as P

LOSS_CELLS = 1024
F32, BF16 = jnp.float32, jnp.bfloat16
W = 48
PITCH = 104
MESH = pl.DeviceIdType.MESH
LON, ZS, GROUPS = 8, 8, 32
S1, S2 = 864, 1296
XS = 4
ROWS = (14, 14, 9)
STARTS = ((0, 13, 27, 40), (0, 13, 27, 40), (0, 9, 18, 27))


def mm(a, b):
    return lax.dot_general(a, b, (((1,), (0,)), ((), ())), preferred_element_type=F32)


def mmt(a, b):
    return lax.dot_general(a, b, (((1,), (1,)), ((), ())), preferred_element_type=F32)


def pieces(size, fold):
    out = []
    for row in range(size * LON // 192):
        at = row * 192
        while at < (row + 1) * 192:
            shard = at // size
            end = min((row + 1) * 192, (shard + 1) * size)
            out.append((shard, at - shard * size, row % fold, 192 * (row // fold) + at - row * 192, end - at))
            at = end
    return out


def group_map():
    moves = [(s, lane, 54 + row, at, n) for s, lane, row, at, n in pieces(S1, 18)]
    for k in range(2):
        moves += [(s, S1 + k * S2 + lane, row, 192 * k + at, n) for s, lane, row, at, n in pieces(S2, 54)]
    return moves


def flat_moves(size, shift):
    out = []
    for piece in range(2):
        lane = 0
        while lane < size:
            at = shift + piece * size + lane
            n = min(size - lane, 192 - at % 192)
            out.append((piece, lane, at // 192, at % 192, n))
            lane += n
    return out


def place():
    lat, lon = lax.axis_index("lat"), lax.axis_index("lon")
    core = lax.rem(lat, 2)
    z = lax.rem(lax.div(lat, 2), ZS)
    yh = lax.div(lat, 2 * ZS)
    x = lax.div(lon, 2)
    yl = lax.rem(lon, 2)
    return lat, lon, yh, z, core, x, yl


def remote(src, dst, send, recv, peer):
    return pltpu.make_async_remote_copy(src_ref=src, dst_ref=dst, send_sem=send, recv_sem=recv,
                                        device_id=peer, device_id_type=MESH)


def level_kernel(w1, w2, w3, x_hbm, c_hbm, feat_ref, gin_ref, o1, o2, o3,
                 x_ref, c_ref, v_ref, vbuf, stage, own, eb, xe, xw, xn, xs, xne, xnw, xse, xsw,
                 ce, cw, cn, cs, cne, cnw, cse, csw, wb, tr,
                 xf, x0, x1, kf2, kf3, kg, k1, k2, k3, cf, hs1, hs2, ds3, ds2, bs, p2, dt, g1, g2, g3, st, il,
                 a3, a2, a1, r3, r2, r1, s3, s2, s1, q3, q2, q1, acc3, acc2, acc1, t3, t2, t1, z3, z2, z1,
                 u3, u2, u1, f3, f2, f1, l3, l2, l1,
                 isem, vsend, vrecv, hsend, hrecv, wsend, wrecv, fsend, psend, precv,
                 a_send, a_recv, x_send, x_recv, z_send, z_recv, y_send, y_recv):
    lat, lon, yh, z, core, x, yl = place()
    last = lax.axis_size("lat") - 1
    east, west = lax.rem(lon + 1, LON), lax.rem(lon + LON - 1, LON)
    north_of, south_of = lax.rem(lat + 31, 32), lax.rem(lat + 1, 32)
    partner = lat + 1 - 2 * core
    across = lax.rem(lat + 16, 32)
    beside = lon + 1 - 2 * yl
    lons = [lax.rem(lon + d, LON) for d in range(1, LON)]
    xq = [lax.rem(x + d, XS) for d in range(XS)]
    zs = [lax.rem(z + d, ZS) for d in range(ZS)]
    def lat_of(half, zz):
        return half * 16 + zz * 2 + core
    near = (1, 7, 2, 6, 3, 5, 4)
    lats = [lat_of(yh, zs[d]) for d in near] + [lat_of(1 - yh, zs[d]) for d in (0, *near)]

    ins = [pltpu.make_async_copy(x_hbm, x_ref, isem.at[0]), pltpu.make_async_copy(c_hbm, c_ref, isem.at[1])]
    for k in ins:
        k.start()
    v_ref[0:1, 0:S1] = w1[...].astype(F32).reshape(1, S1)
    v_ref[0:1, S1 : S1 + S2] = w2[...].astype(F32).reshape(1, S2)
    v_ref[0:1, S1 + S2 :] = w3[...].astype(F32).reshape(1, S2)
    sem = pltpu.get_barrier_semaphore()
    peers = [(lat, p) for p in lons] + [(q, lon) for q in (north_of, south_of, *lats)] + [(across, beside)]
    for peer in peers:
        pl.semaphore_signal(sem, inc=1, device_id=peer, device_id_type=MESH)
    pl.semaphore_wait(sem, len(peers))

    sends = []
    for d in range(1, LON):
        k = remote(v_ref, vbuf.at[lon], vsend.at[d], vrecv.at[lon], (lat, lons[d - 1]))
        k.start()
        sends.append(k)
    halos = []
    def halo(src, dst, peer):
        n = len(halos)
        k = remote(src, dst, hsend.at[n], hrecv.at[n], peer)
        k.start()
        halos.append(k)
        sends.append(k)
    e, w, n, s = (lat, east), (lat, west), (north_of, lon), (south_of, lon)
    halo(x_hbm.at[54:64], xn, s)
    halo(x_hbm.at[0:10], xs, n)
    ins[0].wait()
    for k in range(2):
        il[...] = x_ref[:, 48 * k : 48 * k + 16, :].astype(F32).reshape(1024, 128)
        for j in range(10):
            eb[k, j] = il[pl.ds(j + 6 * k, 64, stride=16), :].astype(BF16)
    halo(eb.at[0], xe, w)
    halo(eb.at[1], xw, e)
    ins[1].wait()

    vbuf[lon] = v_ref[...]
    for d in range(1, LON):
        src = lons[d - 1]
        remote(v_ref, vbuf.at[src], vsend.at[d], vrecv.at[src], (lat, src)).wait_recv()
    for shard, lane, row, at, length in group_map():
        stage[row : row + 1, at : at + length] = vbuf[shard, :, lane : lane + length]
    for t in range(3):
        tr[72 * t : 72 * t + 72, :] = stage[:, 128 * t : 128 * t + 128]
    tr[216:224, :] = jnp.zeros((8, 128), F32)
    for k in range(XS):
        own[k] = tr[56 * k : 56 * k + 56, :].astype(BF16)
    for i, q in enumerate(lats):
        k = remote(own.at[x], wb.at[lat, x], wsend.at[i], wrecv.at[lat, x], (q, lon))
        k.start()
        sends.append(k)
    k = remote(own, wb.at[lat], psend.at[15], precv.at[lat], (partner, lon))
    k.start()
    sends.append(k)
    wb[lat] = own[...]

    north = (lat > 0).astype(F32)
    south = (lat < last).astype(F32)
    def own_row(r, _):
        p = pl.multiple_of((r + 9) * PITCH, 8)
        xf[pl.ds(p + 8, 64), :] = x_ref[r].astype(F32)
        xf[pl.ds(p + 80, 16), :] = jnp.zeros((16, 128), F32)
        return 0
    lax.fori_loop(0, 64, own_row, 0)
    def forward(i):
        q = lats[i]
        remote(own.at[x], wb.at[q, x], wsend.at[i], wrecv.at[q, x], (q, lon)).wait_recv()
        for d in range(1, XS):
            k = remote(wb.at[q, x], wb.at[q, x], fsend.at[i, d], wrecv.at[q, x], (lat, xq[d] * 2 + yl))
            k.start()
            sends.append(k)
    def share(i):
        q = lats[i]
        for d in range(1, XS):
            remote(own.at[x], wb.at[q, xq[d]], fsend.at[i, d], wrecv.at[q, xq[d]], (lat, xq[d] * 2 + yl)).wait_recv()
        k = remote(wb.at[q], wb.at[q], psend.at[i], precv.at[q], (partner, lon))
        k.start()
        sends.append(k)
    for i in range(8):
        forward(i)
    halos[2].wait_recv()
    halos[3].wait_recv()
    halo(xe.at[:, 48:64], xne, s)
    halo(xw.at[:, 48:64], xnw, s)
    halo(xe.at[:, 0:16], xse, n)
    halo(xw.at[:, 0:16], xsw, n)
    for i in range(8, 15):
        forward(i)
    halo(c_ref.at[:, 0:8], ce, w)
    halo(c_ref.at[:, 24:32], cw, e)
    halo(c_ref.at[29:32], cn, s)
    halo(c_ref.at[0:3], cs, n)
    for k in (0, 1, 4, 5, 6, 7):
        halos[k].wait_recv()
    for q in range(9):
        xf[q * PITCH + 8 : q * PITCH + 72, :] = xn[q + 1].astype(F32) * north
        xf[q * PITCH + 80 : q * PITCH + 96, :] = jnp.zeros((16, 128), F32)
    for q in range(10):
        xf[(q + 73) * PITCH + 8 : (q + 73) * PITCH + 72, :] = xs[q].astype(F32) * south
        xf[(q + 73) * PITCH + 80 : (q + 73) * PITCH + 96, :] = jnp.zeros((16, 128), F32)
    for j in range(10):
        for ref, rn, rs, ats in ((xe, xne, xse, (72 + j,)), (xw, xnw, xsw, (94 + j, j - 2))):
            mid = ref[j].astype(F32)
            top = rn[j].astype(F32)[7:16] * north
            low = rs[j].astype(F32)[0:10] * south
            for at in ats:
                if at >= 0:
                    xf[pl.ds(9 * PITCH + at, 64, stride=PITCH), :] = mid
                    xf[pl.ds(at, 9, stride=PITCH), :] = top
                    xf[pl.ds(73 * PITCH + at, 10, stride=PITCH), :] = low
    for i in range(15):
        share(i)
    def split(dst, p, idx):
        for k in range(3):
            dst[idx, :, 128 * k : 128 * k + 128] = xf[pl.ds(p * PITCH + 7 + k, W, stride=2), :].astype(BF16)
    def split_pair(k, _):
        split(x0, 2 * k, k)
        split(x1, 2 * k + 1, k)
        return 0
    lax.fori_loop(0, 41, split_pair, 0)
    split(x0, 82, 41)
    for half in range(2):
        for zz in range(ZS):
            q = half * 16 + zz * 2 + 1 - core
            remote(own, wb.at[q], psend.at[15], precv.at[q], (partner, lon)).wait_recv()

    for g in range(GROUPS):
        for k in range(XS):
            tr[56 * k : 56 * k + 56, :] = wb[g, k].astype(F32)
        at = 54 * g
        kf2[at : at + 54, 0:128] = tr[0:54, :]
        kf2[at : at + 54, 128:192] = tr[72:126, 0:64]
        kf3[at : at + 54, 0:64] = tr[72:126, 64:128]
        kf3[at : at + 54, 64:192] = tr[144:198, :]
        at = 36 * g
        kg[at : at + 18, 0:128] = tr[54:72, :]
        kg[at : at + 18, 128:192] = tr[126:144, 0:64]
        kg[at + 18 : at + 36, 0:64] = tr[126:144, 64:128]
        kg[at + 18 : at + 36, 64:192] = tr[198:216, :]
    k1[...] = kg[...].astype(BF16)
    k2[...] = kf2[...].astype(BF16)
    k3[...] = kf3[...].astype(BF16)

    def rows_ok(start, n, first):
        i = lax.broadcasted_iota(jnp.int32, (n, W, 192), 0) + (start + first)
        glob = i + 32 * lat
        return (glob >= 0) & (glob < 32 * (last + 1))
    def put_shifted(dst, start, n, value):
        dst[1, pl.ds(start, n)] = value.astype(BF16)
        dst[0, pl.ds(start, n)] = pltpu.roll(value, 1, 1).astype(BF16)
        dst[2, pl.ds(start, n)] = pltpu.roll(value, W - 1, 1).astype(BF16)
    def chunks(total, n, body, lo=0, hi=None):
        count = -(-total // n)
        def step(k, _):
            body(jnp.minimum(k * n, total - n))
            return 0
        lax.fori_loop(lo, count if hi is None else hi, step, 0)

    def h_one(s):
        n = 14
        acc = mm(x0[pl.ds(s, n)].reshape(n * W, 384), k1[0:384])
        acc += mm(x1[pl.ds(s, n)].reshape(n * W, 384), k1[384:768])
        acc += mm(x0[pl.ds(s + 1, n)].reshape(n * W, 384), k1[768:1152])
        put_shifted(hs1, s, n, jnp.where(rows_ok(s, n, -4), acc.reshape(n, W, 192), 0.0))
    chunks(41, 14, h_one)

    halos[8].wait_recv()
    halos[9].wait_recv()
    halo(ce.at[29:32], cne, s)
    halo(cw.at[29:32], cnw, s)
    halo(ce.at[0:3], cse, n)
    halo(cw.at[0:3], csw, n)

    def conv(src, k, s, n):
        acc = None
        for a in range(3):
            for b in range(3):
                t = mm(src[b, pl.ds(s + a, n)].reshape(n * W, 192), k[(3 * a + b) * 192 : (3 * a + b + 1) * 192])
                acc = t if acc is None else acc + t
        return acc.reshape(n, W, 192)
    def tconv(src, k, s, n):
        acc = None
        for a in range(3):
            for b in range(3):
                t = mmt(src[2 - b, pl.ds(s + 2 - a, n)].reshape(n * W, 192), k[(3 * a + b) * 192 : (3 * a + b + 1) * 192])
                acc = t if acc is None else acc + t
        return acc.reshape(n, W, 192)

    def h_two(s):
        n = 13
        v = conv(hs1, k2, s, n)
        p2[pl.ds(s, n)] = v
        h = v / (1.0 + jnp.exp(-v))
        put_shifted(hs2, s, n, jnp.where(rows_ok(s, n, -3), h, 0.0))
    chunks(39, 13, h_two)

    for k in halos[10:16]:
        k.wait_recv()
    def cot(idx, row, e, w):
        cf[idx, 0:32, :] = row.astype(F32)
        cf[idx, 32:40, :] = e.astype(F32)
        cf[idx, 40:48, :] = w.astype(F32)
    def cot_own(k, _):
        cot(k + 2, c_ref[k], ce[k], cw[k])
        return 0
    lax.fori_loop(0, 32, cot_own, 0)
    for q in range(2):
        cot(q, cn[q + 1], cne[q + 1], cnw[q + 1])
    for q in range(3):
        cot(q + 34, cs[q], cse[q], csw[q])

    def deriv(v):
        sg = 1.0 / (1.0 + jnp.exp(-v))
        return sg, sg * (1.0 + v * (1.0 - sg))
    def d_three(s):
        n = 13
        v = conv(hs2, k3, s, n)
        sg, dv = deriv(v)
        bs[1, pl.ds(s, n)] = (v * sg).astype(BF16)
        put_shifted(ds3, s, n, jnp.where(rows_ok(s, n, -2), cf[pl.ds(s, n)] * dv, 0.0))
    chunks(37, 13, d_three)
    feat_ref[...] = bs[1, 2:34, 0:32, :]

    def wgrad(src, off, dst):
        for a in range(3):
            for b in range(3):
                win = src[b, off + a : off + a + 32, 0:32, :].reshape(1024, 192)
                t = mm(dt[...], win)
                n0 = (3 * a + b) * 192
                dst[n0 : n0 + 192, :] = t.T
    def to_partner(i, g, a, r):
        rows, group = ROWS[i], 36 if i == 2 else 54
        for zz in range(ZS):
            for c in range(2):
                for q in range(XS):
                    for y in range(2):
                        base = (y * 16 + zz * 2 + c) * group + STARTS[i][q]
                        st[0:rows, 192 * y : 192 * y + 192] = g[base : base + rows, :]
                    a[zz, c, q] = st[0:rows, :].astype(BF16)
        k = remote(a.at[:, 1 - core], r, a_send.at[i], a_recv.at[i], (partner, lon))
        k.start()
        sends.append(k)
        return k
    def along_x(i, k, a, r, sx, qx, acc):
        k.wait_recv()
        for d in (2, 1, 3, 0):
            q = xq[d]
            total = a[:, core, q].astype(F32) + r[:, q].astype(F32)
            if d:
                sx[d] = total.astype(BF16)
                m = remote(sx.at[d], qx.at[x], x_send.at[i, d], x_recv.at[i, x], (lat, q * 2 + yl))
                m.start()
                sends.append(m)
            else:
                acc[...] = total
    def along_z(i, sx, qx, acc, tz, zb):
        for d in (1, 3, 2):
            q = xq[d]
            remote(sx.at[d], qx.at[q], x_send.at[i, d], x_recv.at[i, q], (lat, q * 2 + yl)).wait_recv()
        acc[...] = acc[...] + (qx[xq[1]].astype(F32) + qx[xq[3]].astype(F32)) + qx[xq[2]].astype(F32)
        for d in (4, 3, 5, 2, 6, 1, 7):
            zz = zs[d]
            tz[d] = acc[zz].astype(BF16)
            m = remote(tz.at[d], zb.at[z], z_send.at[i, d], z_recv.at[i, z], (lat_of(yh, zz), lon))
            m.start()
            sends.append(m)
    ys = [(1 - yh, yl, (across, lon)), (yh, 1 - yl, (lat, beside)), (1 - yh, 1 - yl, (across, beside))]
    def along_y(i, acc, tz, zb, u, f, l):
        size = S1 if i == 2 else S2
        total = acc[z]
        for d in near:
            zz = zs[d]
            remote(tz.at[d], zb.at[zz], z_send.at[i, d], z_recv.at[i, zz], (lat_of(yh, zz), lon)).wait_recv()
            total = total + zb[zz].astype(F32)
        u[...] = total
        def cut(shift):
            for y in range(2):
                for piece, lane, row, at, length in flat_moves(size, shift):
                    f[2 * y + piece, :, lane : lane + length] = u[row : row + 1, 192 * y + at : 192 * y + at + length]
        if i == 2:
            cut(0)
        else:
            @pl.when(lax.rem(x, 2) == 0)
            def _():
                cut(0)
            @pl.when(lax.rem(x, 2) == 1)
            def _():
                cut(96)
        me = 2 * yh + yl
        for d, (h, b, peer) in enumerate(ys):
            m = remote(f.at[2 * h + b], l.at[me], y_send.at[i, d], y_recv.at[i, me], peer)
            m.start()
            sends.append(m)
        l[me] = f[me]
    def total_of(i, f, l):
        for d, (h, b, peer) in enumerate(ys):
            remote(f.at[2 * h + b], l.at[2 * h + b], y_send.at[i, d], y_recv.at[i, 2 * h + b], peer).wait_recv()
        return (((l[0] + l[1]) + (l[2] + l[3])) * (1.0 / LOSS_CELLS)).reshape(S1 if i == 2 else S2)

    dt[...] = ds3[1, 2:34, 0:32, :].reshape(1024, 192).T
    wgrad(hs2, 2, g3)
    c3 = to_partner(0, g3, a3, r3)

    def d_two(s):
        n = 12
        v = tconv(ds3, k3, s, n)
        _, dv = deriv(p2[pl.ds(s + 2, n)])
        put_shifted(ds2, s, n, jnp.where(rows_ok(s, n, -1), v * dv, 0.0))
    chunks(35, 12, d_two)
    along_x(0, c3, a3, r3, s3, q3, acc3)
    dt[...] = ds2[1, 1:33, 0:32, :].reshape(1024, 192).T
    wgrad(hs1, 3, g2)
    c2 = to_partner(1, g2, a2, r2)

    def b_one(s):
        n = 11
        v = jnp.where(rows_ok(s, n, 0), tconv(ds2, k2, s, n), 0.0)
        bs[1, pl.ds(s, n)] = v.astype(BF16)
        bs[2, pl.ds(s, n)] = pltpu.roll(v, W - 1, 1).astype(BF16)
    chunks(33, 11, b_one, 0, 1)
    along_x(1, c2, a2, r2, s2, q2, acc2)
    chunks(33, 11, b_one, 1, 2)
    along_z(0, s3, q3, acc3, t3, z3)
    chunks(33, 11, b_one, 2, 3)
    dt[...] = bs[1, 0:32, 0:32, :].reshape(1024, 192).T
    for a in range(3):
        src = x1 if a == 1 else x0
        off = 4 + (a == 2)
        win = src[off : off + 32, 0:32, :].reshape(1024, 384)
        g1[384 * a : 384 * a + 384, :] = mm(dt[...], win).T
    c1 = to_partner(2, g1, a1, r1)
    along_z(1, s2, q2, acc2, t2, z2)
    def k1t(a, b):
        n0 = (3 * a + b) * 128
        return k1[n0 : n0 + 128]
    def gin(i):
        n = 8
        here = bs[1, pl.ds(i, n), 0:32, :].reshape(n * 32, 192)
        right = bs[2, pl.ds(i, n), 0:32, :].reshape(n * 32, 192)
        below = bs[1, pl.ds(i + 1, n), 0:32, :].reshape(n * 32, 192)
        corner = bs[2, pl.ds(i + 1, n), 0:32, :].reshape(n * 32, 192)
        ee = mmt(here, k1t(1, 1))
        eo = mmt(right, k1t(1, 0)) + mmt(here, k1t(1, 2))
        oe = mmt(below, k1t(0, 1)) + mmt(here, k1t(2, 1))
        oo = mmt(corner, k1t(0, 0)) + mmt(below, k1t(0, 2)) + mmt(right, k1t(2, 0)) + mmt(here, k1t(2, 2))
        il[pl.ds(0, n * 32, stride=2), :] = ee
        il[pl.ds(1, n * 32, stride=2), :] = eo
        il[pl.ds(n * 64, n * 32, stride=2), :] = oe
        il[pl.ds(n * 64 + 1, n * 32, stride=2), :] = oo
        even = il[0 : n * 64, :].reshape(n, 64, 128).astype(BF16)
        odd = il[n * 64 : n * 128, :].reshape(n, 64, 128).astype(BF16)
        for m in range(n):
            gin_ref[2 * (i + m)] = even[m]
            gin_ref[2 * (i + m) + 1] = odd[m]
    chunks(32, 8, gin, 0, 1)
    along_x(2, c1, a1, r1, s1, q1, acc1)
    chunks(32, 8, gin, 1, 4)
    along_y(0, acc3, t3, z3, u3, f3, l3)
    along_z(2, s1, q1, acc1, t1, z1)
    along_y(1, acc2, t2, z2, u2, f2, l2)
    o3[...] = total_of(0, f3, l3)
    o2[...] = total_of(1, f2, l2)
    along_y(2, acc1, t1, z1, u1, f1, l1)
    o1[...] = total_of(2, f1, l1)
    for k in sends:
        k.wait_send()


def level(w1, w2, w3, x, c):
    V, D = pltpu.VMEM, pltpu.SemaphoreType.DMA
    vm = pl.BlockSpec(memory_space=pltpu.VMEM)
    hbm = pl.BlockSpec(memory_space=pl.ANY)
    sds = jax.ShapeDtypeStruct
    def each(shape_of, dtype=BF16):
        return [V(shape_of(r), dtype) for r in ROWS]
    def flats():
        return [V((4, 1, n), F32) for n in (S2, S2, S1)]
    halos = [(10, 64, 128)] * 4 + [(10, 16, 128)] * 4 + [(32, 8, 192)] * 2 + [(3, 32, 192)] * 2 + [(3, 8, 192)] * 4
    return pl.pallas_call(
        level_kernel,
        out_shape=(sds((32, 32, 192), BF16), sds((64, 64, 128), BF16), sds((S1,), F32), sds((S2,), F32), sds((S2,), F32)),
        in_specs=[vm, vm, vm, hbm, hbm],
        out_specs=(vm,) * 5,
        scratch_shapes=[
            V((64, 64, 128), BF16), V((32, 32, 192), BF16), V((1, 3456), F32), V((LON, 1, 3456), F32), V((72, 384), F32),
            V((XS, 56, 128), BF16), V((2, 10, 64, 128), BF16), *[V(s, BF16) for s in halos],
            V((GROUPS, XS, 56, 128), BF16), V((224, 128), F32),
            V((83 * PITCH, 128), F32), V((42, W, 384), BF16), V((42, W, 384), BF16),
            V((1728, 192), F32), V((1728, 192), F32), V((1152, 192), F32),
            V((1152, 192), BF16), V((1728, 192), BF16), V((1728, 192), BF16),
            V((37, W, 192), F32), V((3, 41, W, 192), BF16), V((3, 39, W, 192), BF16),
            V((3, 37, W, 192), BF16), V((3, 35, W, 192), BF16), V((3, 37, W, 192), BF16),
            V((39, W, 192), F32), V((192, 1024), BF16), V((1152, 192), F32), V((1728, 192), F32), V((1728, 192), F32),
            V((14, 384), F32), V((1024, 128), F32),
            *each(lambda r: (ZS, 2, XS, r, 384)), *each(lambda r: (ZS, XS, r, 384)),
            *each(lambda r: (XS, ZS, r, 384)), *each(lambda r: (XS, ZS, r, 384)),
            *each(lambda r: (ZS, r, 384), F32), *each(lambda r: (ZS, r, 384)), *each(lambda r: (ZS, r, 384)),
            *each(lambda r: (r, 384), F32), *flats(), *flats(),
            D((2,)), D((LON,)), D((LON,)), D((20,)), D((20,)), D((16,)), D((GROUPS, XS)), D((16, XS)), D((16,)), D((GROUPS,)),
            D((3,)), D((3,)), D((3, XS)), D((3, XS)), D((3, ZS)), D((3, ZS)), D((3, 4)), D((3, 4)),
        ],
        compiler_params=pltpu.CompilerParams(collective_id=0, has_side_effects=True, vmem_limit_bytes=63 * 1024 * 1024),
        name="level",
    )(w1, w2, w3, x, c)


def finish_kernel(f, g, a, b, c, fo, go, ao, bo, co, fv, gv, av, bv, cv, isem, osem):
    trips = [(f, fv, fo), (a, av, ao), (b, bv, bo), (c, cv, co)]
    trips += [(g.at[16 * k : 16 * k + 16], gv.at[16 * k : 16 * k + 16], go.at[16 * k : 16 * k + 16]) for k in range(4)]
    ins = [pltpu.make_async_copy(src, mid, isem.at[i]) for i, (src, mid, _) in enumerate(trips)]
    outs = [pltpu.make_async_copy(mid, dst, osem.at[i]) for i, (_, mid, dst) in enumerate(trips)]
    for k in ins:
        k.start()
    for k, m in zip(ins, outs):
        k.wait()
        m.start()
    for m in outs:
        m.wait()


def finish(*arrays):
    hbm = pl.BlockSpec(memory_space=pl.ANY)
    return pl.pallas_call(
        finish_kernel,
        out_shape=tuple(jax.ShapeDtypeStruct(a.shape, a.dtype) for a in arrays),
        in_specs=[hbm] * 5,
        out_specs=(hbm,) * 5,
        scratch_shapes=[*[pltpu.VMEM(a.shape, a.dtype) for a in arrays],
                        pltpu.SemaphoreType.DMA((8,)), pltpu.SemaphoreType.DMA((8,))],
        name="results",
    )(*arrays)


def local(inputs, w_first, w_second, w_third, cotangent):
    return finish(*level(w_first, w_second, w_third, inputs, cotangent))


def solution(mesh):
    tile, flat = P("lat", "lon", None), P(("lat", "lon"))
    return jax.shard_map(
        local,
        mesh=mesh,
        in_specs=(tile, flat, flat, flat, tile),
        out_specs=(tile, tile, flat, flat, flat),
        check_vma=False,
    )
```

```python
import jax
import jax.numpy as jnp
from jax import lax
from jax.experimental import pallas as pl
from jax.experimental.pallas import tpu as pltpu
from jax.sharding import PartitionSpec as P

LOSS_CELLS = 1024
F32, BF16 = jnp.float32, jnp.bfloat16
W = 48
PITCH = 104
MESH = pl.DeviceIdType.MESH
LON, ZS, GROUPS = 8, 8, 32
S1, S2 = 864, 1296
XS = 4
ROWS = (14, 14, 9)
PACKED = (48, 48, 32)
ORDER = (4, 3, 5, 2, 6, 1, 7, 0)
STARTS = ((0, 13, 27, 40), (0, 13, 27, 40), (0, 9, 18, 27))


def mm(a, b):
    return lax.dot_general(a, b, (((1,), (0,)), ((), ())), preferred_element_type=F32)


def mmt(a, b):
    return lax.dot_general(a, b, (((1,), (1,)), ((), ())), preferred_element_type=F32)


def pieces(size, fold):
    out = []
    for row in range(size * LON // 192):
        at = row * 192
        while at < (row + 1) * 192:
            shard = at // size
            end = min((row + 1) * 192, (shard + 1) * size)
            out.append((shard, at - shard * size, row % fold, 192 * (row // fold) + at - row * 192, end - at))
            at = end
    return out


def group_map():
    moves = [(s, lane, 54 + row, at, n) for s, lane, row, at, n in pieces(S1, 18)]
    for k in range(2):
        moves += [(s, S1 + k * S2 + lane, row, 192 * k + at, n) for s, lane, row, at, n in pieces(S2, 54)]
    return moves


def flat_moves(size, shift, rows, y):
    out = []
    for piece in range(2):
        lane = 0
        while lane < size:
            at = shift + piece * size + lane
            row, col = at // 192, at % 192
            n = min(size - lane, (128 if col < 128 else 192) - col)
            spot = (y * rows + row, col) if col < 128 else (2 * rows + row, 64 * y + col - 128)
            out.append((piece, lane, *spot, n))
            lane += n
    return out


def place():
    lat, lon = lax.axis_index("lat"), lax.axis_index("lon")
    core = lax.rem(lat, 2)
    z = lax.rem(lax.div(lat, 2), ZS)
    yh = lax.div(lat, 2 * ZS)
    x = lax.div(lon, 2)
    yl = lax.rem(lon, 2)
    return lat, lon, yh, z, core, x, yl


def remote(src, dst, send, recv, peer):
    return pltpu.make_async_remote_copy(src_ref=src, dst_ref=dst, send_sem=send, recv_sem=recv,
                                        device_id=peer, device_id_type=MESH)


def level_kernel(w1, w2, w3, x_hbm, c_hbm, feat_ref, gin_ref, o1, o2, o3,
                 x_ref, c_ref, v_ref, vbuf, stage, own, eb, xe, xw, xn, xs, xne, xnw, xse, xsw,
                 ce, cw, cn, cs, cne, cnw, cse, csw, wb, tr,
                 xf, x0, x1, kf2, kf3, kg, k1, k2, k3, cf, hs1, hs2, ds3, ds2, bs, p2, dt, g1, g2, g3, st, il,
                 a3, a2, a1, r3, r2, r1, s3, s2, s1, q3, q2, q1, acc3, acc2, acc1, t3, t2, t1, z3, z2, z1,
                 u3, u2, u1, f3, f2, f1, l3, l2, l1,
                 isem, vsend, vrecv, hsend, hrecv, wsend, wrecv, fsend, psend, precv,
                 a_send, a_recv, x_send, x_recv, z_send, z_recv, y_send, y_recv):
    lat, lon, yh, z, core, x, yl = place()
    last = lax.axis_size("lat") - 1
    east, west = lax.rem(lon + 1, LON), lax.rem(lon + LON - 1, LON)
    north_of, south_of = lax.rem(lat + 31, 32), lax.rem(lat + 1, 32)
    partner = lat + 1 - 2 * core
    across = lax.rem(lat + 16, 32)
    beside = lon + 1 - 2 * yl
    lons = [lax.rem(lon + d, LON) for d in range(1, LON)]
    xq = [lax.rem(x + d, XS) for d in range(XS)]
    zs = [lax.rem(z + d, ZS) for d in range(ZS)]
    def lat_of(half, zz):
        return half * 16 + zz * 2 + core
    near = (1, 7, 2, 6, 3, 5, 4)
    lats = [lat_of(yh, zs[d]) for d in near] + [lat_of(1 - yh, zs[d]) for d in (0, *near)]

    ins = [pltpu.make_async_copy(x_hbm, x_ref, isem.at[0]), pltpu.make_async_copy(c_hbm, c_ref, isem.at[1])]
    for k in ins:
        k.start()
    v_ref[0:1, 0:S1] = w1[...].astype(F32).reshape(1, S1)
    v_ref[0:1, S1 : S1 + S2] = w2[...].astype(F32).reshape(1, S2)
    v_ref[0:1, S1 + S2 :] = w3[...].astype(F32).reshape(1, S2)
    sem = pltpu.get_barrier_semaphore()
    peers = [(lat, p) for p in lons] + [(q, lon) for q in (north_of, south_of, *lats)] + [(across, beside)]
    for peer in peers:
        pl.semaphore_signal(sem, inc=1, device_id=peer, device_id_type=MESH)
    pl.semaphore_wait(sem, len(peers))

    sends = []
    for d in range(1, LON):
        k = remote(v_ref, vbuf.at[lon], vsend.at[d], vrecv.at[lon], (lat, lons[d - 1]))
        k.start()
        sends.append(k)
    halos = []
    def halo(src, dst, peer):
        n = len(halos)
        k = remote(src, dst, hsend.at[n], hrecv.at[n], peer)
        k.start()
        halos.append(k)
        sends.append(k)
    e, w, n, s = (lat, east), (lat, west), (north_of, lon), (south_of, lon)
    halo(x_hbm.at[54:64], xn, s)
    halo(x_hbm.at[0:10], xs, n)
    ins[0].wait()
    for k in range(2):
        il[...] = x_ref[:, 48 * k : 48 * k + 16, :].astype(F32).reshape(1024, 128)
        for j in range(10):
            eb[k, j] = il[pl.ds(j + 6 * k, 64, stride=16), :].astype(BF16)
    halo(eb.at[0], xe, w)
    halo(eb.at[1], xw, e)
    ins[1].wait()

    vbuf[lon] = v_ref[...]
    for d in range(1, LON):
        src = lons[d - 1]
        remote(v_ref, vbuf.at[src], vsend.at[d], vrecv.at[src], (lat, src)).wait_recv()
    for shard, lane, row, at, length in group_map():
        stage[row : row + 1, at : at + length] = vbuf[shard, :, lane : lane + length]
    for t in range(3):
        tr[72 * t : 72 * t + 72, :] = stage[:, 128 * t : 128 * t + 128]
    tr[216:224, :] = jnp.zeros((8, 128), F32)
    for k in range(XS):
        own[k] = tr[56 * k : 56 * k + 56, :].astype(BF16)
    for i, q in enumerate(lats):
        k = remote(own.at[x], wb.at[lat, x], wsend.at[i], wrecv.at[lat, x], (q, lon))
        k.start()
        sends.append(k)
    k = remote(own, wb.at[lat], psend.at[15], precv.at[lat], (partner, lon))
    k.start()
    sends.append(k)
    wb[lat] = own[...]

    halo(c_ref.at[:, 0:8], ce, w)
    halo(c_ref.at[:, 24:32], cw, e)
    halo(c_ref.at[29:32], cn, s)
    halo(c_ref.at[0:3], cs, n)

    north = (lat > 0).astype(F32)
    south = (lat < last).astype(F32)
    def own_row(r, _):
        p = pl.multiple_of((r + 9) * PITCH, 8)
        xf[pl.ds(p + 8, 64), :] = x_ref[r].astype(F32)
        xf[pl.ds(p + 80, 16), :] = jnp.zeros((16, 128), F32)
        return 0
    lax.fori_loop(0, 64, own_row, 0)
    def forward(i):
        q = lats[i]
        remote(own.at[x], wb.at[q, x], wsend.at[i], wrecv.at[q, x], (q, lon)).wait_recv()
        for d in range(1, XS):
            k = remote(wb.at[q, x], wb.at[q, x], fsend.at[i, d], wrecv.at[q, x], (lat, xq[d] * 2 + yl))
            k.start()
            sends.append(k)
    def share(i):
        q = lats[i]
        for d in range(1, XS):
            remote(own.at[x], wb.at[q, xq[d]], fsend.at[i, d], wrecv.at[q, xq[d]], (lat, xq[d] * 2 + yl)).wait_recv()
        k = remote(wb.at[q], wb.at[q], psend.at[i], precv.at[q], (partner, lon))
        k.start()
        sends.append(k)
    for i in range(15):
        forward(i)
    halos[2].wait_recv()
    halos[3].wait_recv()
    halo(xe.at[:, 48:64], xne, s)
    halo(xw.at[:, 48:64], xnw, s)
    halo(xe.at[:, 0:16], xse, n)
    halo(xw.at[:, 0:16], xsw, n)
    sides = [(xe, xne, xse, (72 + j,), j) for j in range(10)] + [(xw, xnw, xsw, (94 + j, j - 2), j) for j in range(10)]
    for ref, rn, rs, ats, j in sides:
        for at in ats:
            if at >= 0:
                xf[pl.ds(9 * PITCH + at, 64, stride=PITCH), :] = ref[j].astype(F32)
    for i in range(5):
        share(i)
    def split(dst, p, idx):
        for k in range(3):
            dst[idx, :, 128 * k : 128 * k + 128] = xf[pl.ds(p * PITCH + 7 + k, W, stride=2), :].astype(BF16)
    def split_pair(k, _):
        split(x0, 2 * k, k)
        split(x1, 2 * k + 1, k)
        return 0
    lax.fori_loop(5, 36, split_pair, 0)
    for i in range(5, 10):
        share(i)
    for k in (0, 1, 8, 9, 10, 11):
        halos[k].wait_recv()
    for q in range(9):
        xf[q * PITCH + 8 : q * PITCH + 72, :] = xn[q + 1].astype(F32) * north
        xf[q * PITCH + 80 : q * PITCH + 96, :] = jnp.zeros((16, 128), F32)
    for q in range(10):
        xf[(q + 73) * PITCH + 8 : (q + 73) * PITCH + 72, :] = xs[q].astype(F32) * south
        xf[(q + 73) * PITCH + 80 : (q + 73) * PITCH + 96, :] = jnp.zeros((16, 128), F32)
    for ref, rn, rs, ats, j in sides:
        top = rn[j].astype(F32)[7:16] * north
        low = rs[j].astype(F32)[0:10] * south
        for at in ats:
            if at >= 0:
                xf[pl.ds(at, 9, stride=PITCH), :] = top
                xf[pl.ds(73 * PITCH + at, 10, stride=PITCH), :] = low
    for i in range(10, 15):
        share(i)
    lax.fori_loop(0, 5, split_pair, 0)
    lax.fori_loop(36, 41, split_pair, 0)
    split(x0, 82, 41)
    for half in range(2):
        for zz in range(ZS):
            q = half * 16 + zz * 2 + 1 - core
            remote(own, wb.at[q], psend.at[15], precv.at[q], (partner, lon)).wait_recv()

    for g in range(GROUPS):
        for k in range(XS):
            tr[56 * k : 56 * k + 56, :] = wb[g, k].astype(F32)
        at = 54 * g
        kf2[at : at + 54, 0:128] = tr[0:54, :]
        kf2[at : at + 54, 128:192] = tr[72:126, 0:64]
        kf3[at : at + 54, 0:64] = tr[72:126, 64:128]
        kf3[at : at + 54, 64:192] = tr[144:198, :]
        at = 36 * g
        kg[at : at + 18, 0:128] = tr[54:72, :]
        kg[at : at + 18, 128:192] = tr[126:144, 0:64]
        kg[at + 18 : at + 36, 0:64] = tr[126:144, 64:128]
        kg[at + 18 : at + 36, 64:192] = tr[198:216, :]
    k1[...] = kg[...].astype(BF16)
    k2[...] = kf2[...].astype(BF16)
    k3[...] = kf3[...].astype(BF16)

    def rows_ok(start, n, first):
        i = lax.broadcasted_iota(jnp.int32, (n, W, 192), 0) + (start + first)
        glob = i + 32 * lat
        return (glob >= 0) & (glob < 32 * (last + 1))
    def put_shifted(dst, start, n, value):
        dst[1, pl.ds(start, n)] = value.astype(BF16)
        dst[0, pl.ds(start, n)] = pltpu.roll(value, 1, 1).astype(BF16)
        dst[2, pl.ds(start, n)] = pltpu.roll(value, W - 1, 1).astype(BF16)
    def chunks(total, n, body, lo=0, hi=None):
        count = -(-total // n)
        def step(k, _):
            body(jnp.minimum(k * n, total - n))
            return 0
        lax.fori_loop(lo, count if hi is None else hi, step, 0)

    def h_one(s):
        n = 14
        acc = mm(x0[pl.ds(s, n)].reshape(n * W, 384), k1[0:384])
        acc += mm(x1[pl.ds(s, n)].reshape(n * W, 384), k1[384:768])
        acc += mm(x0[pl.ds(s + 1, n)].reshape(n * W, 384), k1[768:1152])
        put_shifted(hs1, s, n, jnp.where(rows_ok(s, n, -4), acc.reshape(n, W, 192), 0.0))
    chunks(41, 14, h_one)

    halos[4].wait_recv()
    halos[5].wait_recv()
    halo(ce.at[29:32], cne, s)
    halo(cw.at[29:32], cnw, s)
    halo(ce.at[0:3], cse, n)
    halo(cw.at[0:3], csw, n)

    def conv(src, k, s, n):
        acc = None
        for a in range(3):
            for b in range(3):
                t = mm(src[b, pl.ds(s + a, n)].reshape(n * W, 192), k[(3 * a + b) * 192 : (3 * a + b + 1) * 192])
                acc = t if acc is None else acc + t
        return acc.reshape(n, W, 192)
    def tconv(src, k, s, n):
        acc = None
        for a in range(3):
            for b in range(3):
                t = mmt(src[2 - b, pl.ds(s + 2 - a, n)].reshape(n * W, 192), k[(3 * a + b) * 192 : (3 * a + b + 1) * 192])
                acc = t if acc is None else acc + t
        return acc.reshape(n, W, 192)

    def h_two(s):
        n = 13
        v = conv(hs1, k2, s, n)
        p2[pl.ds(s, n)] = v
        h = v / (1.0 + jnp.exp(-v))
        put_shifted(hs2, s, n, jnp.where(rows_ok(s, n, -3), h, 0.0))
    chunks(39, 13, h_two)

    for k in halos[6:8] + halos[12:16]:
        k.wait_recv()
    def cot(idx, row, e, w):
        cf[idx, 0:32, :] = row.astype(F32)
        cf[idx, 32:40, :] = e.astype(F32)
        cf[idx, 40:48, :] = w.astype(F32)
    def cot_own(k, _):
        cot(k + 2, c_ref[k], ce[k], cw[k])
        return 0
    lax.fori_loop(0, 32, cot_own, 0)
    for q in range(2):
        cot(q, cn[q + 1], cne[q + 1], cnw[q + 1])
    for q in range(3):
        cot(q + 34, cs[q], cse[q], csw[q])

    def deriv(v):
        sg = 1.0 / (1.0 + jnp.exp(-v))
        return sg, sg * (1.0 + v * (1.0 - sg))
    def d_three(s):
        n = 13
        v = conv(hs2, k3, s, n)
        sg, dv = deriv(v)
        bs[1, pl.ds(s, n)] = (v * sg).astype(BF16)
        put_shifted(ds3, s, n, jnp.where(rows_ok(s, n, -2), cf[pl.ds(s, n)] * dv, 0.0))
    chunks(37, 13, d_three)
    feat_ref[...] = bs[1, 2:34, 0:32, :]

    def wgrad(src, off, dst):
        for a in range(3):
            for b in range(3):
                win = src[b, off + a : off + a + 32, 0:32, :].reshape(1024, 192)
                t = mm(dt[...], win)
                n0 = (3 * a + b) * 192
                dst[n0 : n0 + 192, :] = t.T
    st[...] = jnp.zeros_like(st)
    def to_partner(i, g, a, r):
        rows, group = ROWS[i], 36 if i == 2 else 54
        for zz in range(ZS):
            for c in range(2):
                for q in range(XS):
                    for y in range(2):
                        base = (y * 16 + zz * 2 + c) * group + STARTS[i][q]
                        st[y * rows : (y + 1) * rows, :] = g[base : base + rows, 0:128]
                        st[2 * rows : 3 * rows, 64 * y : 64 * y + 64] = g[base : base + rows, 128:192]
                    a[zz, c, q] = st[0 : PACKED[i], :].astype(BF16)
        k = remote(a.at[:, 1 - core], r, a_send.at[i], a_recv.at[i], (partner, lon))
        k.start()
        sends.append(k)
        return k
    def along_x(i, k, a, r, sx, qx, acc):
        k.wait_recv()
        for half in range(2):
            for d in (2, 1, 3, 0):
                q = xq[d]
                for p in range(4 * half, 4 * half + 4):
                    zz = zs[ORDER[p]]
                    total = a[zz, core, q].astype(F32) + r[zz, q].astype(F32)
                    if d:
                        sx[d, p] = total.astype(BF16)
                    else:
                        acc[p] = total
                if d:
                    part = pl.ds(4 * half, 4)
                    m = remote(sx.at[d, part], qx.at[x, part], x_send.at[i, d, half], x_recv.at[i, x, half], (lat, q * 2 + yl))
                    m.start()
                    sends.append(m)
    def along_z(i, sx, qx, acc, tz, zb):
        for half in range(2):
            part = pl.ds(4 * half, 4)
            for d in (1, 3, 2):
                q = xq[d]
                remote(sx.at[d, part], qx.at[q, part], x_send.at[i, d, half], x_recv.at[i, q, half], (lat, q * 2 + yl)).wait_recv()
            for p in range(4 * half, 4 * half + 4):
                d = ORDER[p]
                total = acc[p] + (qx[xq[1], p].astype(F32) + qx[xq[3], p].astype(F32)) + qx[xq[2], p].astype(F32)
                if d:
                    tz[d] = total.astype(BF16)
                    m = remote(tz.at[d], zb.at[z], z_send.at[i, d], z_recv.at[i, z], (lat_of(yh, zs[d]), lon))
                    m.start()
                    sends.append(m)
                else:
                    acc[p] = total
    ys = [(1 - yh, yl, (across, lon)), (yh, 1 - yl, (lat, beside)), (1 - yh, 1 - yl, (across, beside))]
    def along_y(i, acc, tz, zb, u, f, l):
        size = S1 if i == 2 else S2
        total = acc[7]
        for d in near:
            zz = zs[d]
            remote(tz.at[d], zb.at[zz], z_send.at[i, d], z_recv.at[i, zz], (lat_of(yh, zz), lon)).wait_recv()
            total = total + zb[zz].astype(F32)
        u[...] = total
        def cut(shift):
            for y in range(2):
                for piece, lane, row, at, length in flat_moves(size, shift, ROWS[i], y):
                    f[2 * y + piece, :, lane : lane + length] = u[row : row + 1, at : at + length]
        if i == 2:
            cut(0)
        else:
            @pl.when(lax.rem(x, 2) == 0)
            def _():
                cut(0)
            @pl.when(lax.rem(x, 2) == 1)
            def _():
                cut(96)
        me = 2 * yh + yl
        for d, (h, b, peer) in enumerate(ys):
            m = remote(f.at[2 * h + b], l.at[me], y_send.at[i, d], y_recv.at[i, me], peer)
            m.start()
            sends.append(m)
        l[me] = f[me]
    def total_of(i, f, l):
        for d, (h, b, peer) in enumerate(ys):
            remote(f.at[2 * h + b], l.at[2 * h + b], y_send.at[i, d], y_recv.at[i, 2 * h + b], peer).wait_recv()
        return (((l[0] + l[1]) + (l[2] + l[3])) * (1.0 / LOSS_CELLS)).reshape(S1 if i == 2 else S2)

    dt[...] = ds3[1, 2:34, 0:32, :].reshape(1024, 192).T
    wgrad(hs2, 2, g3)
    c3 = to_partner(0, g3, a3, r3)

    def d_two(s):
        n = 12
        v = tconv(ds3, k3, s, n)
        _, dv = deriv(p2[pl.ds(s + 2, n)])
        put_shifted(ds2, s, n, jnp.where(rows_ok(s, n, -1), v * dv, 0.0))
    chunks(35, 12, d_two)
    along_x(0, c3, a3, r3, s3, q3, acc3)
    dt[...] = ds2[1, 1:33, 0:32, :].reshape(1024, 192).T
    wgrad(hs1, 3, g2)
    c2 = to_partner(1, g2, a2, r2)

    def b_one(s):
        n = 11
        v = jnp.where(rows_ok(s, n, 0), tconv(ds2, k2, s, n), 0.0)
        bs[1, pl.ds(s, n)] = v.astype(BF16)
        bs[2, pl.ds(s, n)] = pltpu.roll(v, W - 1, 1).astype(BF16)
    chunks(33, 11, b_one, 0, 1)
    along_x(1, c2, a2, r2, s2, q2, acc2)
    chunks(33, 11, b_one, 1, 2)
    along_z(0, s3, q3, acc3, t3, z3)
    chunks(33, 11, b_one, 2, 3)
    dt[...] = bs[1, 0:32, 0:32, :].reshape(1024, 192).T
    for a in range(3):
        src = x1 if a == 1 else x0
        off = 4 + (a == 2)
        win = src[off : off + 32, 0:32, :].reshape(1024, 384)
        g1[384 * a : 384 * a + 384, :] = mm(dt[...], win).T
    c1 = to_partner(2, g1, a1, r1)
    along_z(1, s2, q2, acc2, t2, z2)
    def k1t(a, b):
        n0 = (3 * a + b) * 128
        return k1[n0 : n0 + 128]
    def gin(i):
        n = 8
        here = bs[1, pl.ds(i, n), 0:32, :].reshape(n * 32, 192)
        right = bs[2, pl.ds(i, n), 0:32, :].reshape(n * 32, 192)
        below = bs[1, pl.ds(i + 1, n), 0:32, :].reshape(n * 32, 192)
        corner = bs[2, pl.ds(i + 1, n), 0:32, :].reshape(n * 32, 192)
        ee = mmt(here, k1t(1, 1))
        eo = mmt(right, k1t(1, 0)) + mmt(here, k1t(1, 2))
        oe = mmt(below, k1t(0, 1)) + mmt(here, k1t(2, 1))
        oo = mmt(corner, k1t(0, 0)) + mmt(below, k1t(0, 2)) + mmt(right, k1t(2, 0)) + mmt(here, k1t(2, 2))
        il[pl.ds(0, n * 32, stride=2), :] = ee
        il[pl.ds(1, n * 32, stride=2), :] = eo
        il[pl.ds(n * 64, n * 32, stride=2), :] = oe
        il[pl.ds(n * 64 + 1, n * 32, stride=2), :] = oo
        even = il[0 : n * 64, :].reshape(n, 64, 128).astype(BF16)
        odd = il[n * 64 : n * 128, :].reshape(n, 64, 128).astype(BF16)
        for m in range(n):
            gin_ref[2 * (i + m)] = even[m]
            gin_ref[2 * (i + m) + 1] = odd[m]
    chunks(32, 8, gin, 0, 1)
    along_x(2, c1, a1, r1, s1, q1, acc1)
    chunks(32, 8, gin, 1, 4)
    along_z(2, s1, q1, acc1, t1, z1)
    along_y(0, acc3, t3, z3, u3, f3, l3)
    along_y(1, acc2, t2, z2, u2, f2, l2)
    o3[...] = total_of(0, f3, l3)
    o2[...] = total_of(1, f2, l2)
    along_y(2, acc1, t1, z1, u1, f1, l1)
    o1[...] = total_of(2, f1, l1)
    for k in sends:
        k.wait_send()


def level(w1, w2, w3, x, c):
    V, D = pltpu.VMEM, pltpu.SemaphoreType.DMA
    vm = pl.BlockSpec(memory_space=pltpu.VMEM)
    hbm = pl.BlockSpec(memory_space=pl.ANY)
    sds = jax.ShapeDtypeStruct
    def each(shape_of, dtype=BF16):
        return [V(shape_of(r), dtype) for r in PACKED]
    def flats():
        return [V((4, 1, n), F32) for n in (S2, S2, S1)]
    halos = [(10, 64, 128)] * 4 + [(10, 16, 128)] * 4 + [(32, 8, 192)] * 2 + [(3, 32, 192)] * 2 + [(3, 8, 192)] * 4
    return pl.pallas_call(
        level_kernel,
        out_shape=(sds((32, 32, 192), BF16), sds((64, 64, 128), BF16), sds((S1,), F32), sds((S2,), F32), sds((S2,), F32)),
        in_specs=[vm, vm, vm, hbm, hbm],
        out_specs=(vm,) * 5,
        scratch_shapes=[
            V((64, 64, 128), BF16), V((32, 32, 192), BF16), V((1, 3456), F32), V((LON, 1, 3456), F32), V((72, 384), F32),
            V((XS, 56, 128), BF16), V((2, 10, 64, 128), BF16), *[V(s, BF16) for s in halos],
            V((GROUPS, XS, 56, 128), BF16), V((224, 128), F32),
            V((83 * PITCH, 128), F32), V((42, W, 384), BF16), V((42, W, 384), BF16),
            V((1728, 192), F32), V((1728, 192), F32), V((1152, 192), F32),
            V((1152, 192), BF16), V((1728, 192), BF16), V((1728, 192), BF16),
            V((37, W, 192), F32), V((3, 41, W, 192), BF16), V((3, 39, W, 192), BF16),
            V((3, 37, W, 192), BF16), V((3, 35, W, 192), BF16), V((3, 37, W, 192), BF16),
            V((39, W, 192), F32), V((192, 1024), BF16), V((1152, 192), F32), V((1728, 192), F32), V((1728, 192), F32),
            V((48, 128), F32), V((1024, 128), F32),
            *each(lambda r: (ZS, 2, XS, r, 128)), *each(lambda r: (ZS, XS, r, 128)),
            *each(lambda r: (XS, ZS, r, 128)), *each(lambda r: (XS, ZS, r, 128)),
            *each(lambda r: (ZS, r, 128), F32), *each(lambda r: (ZS, r, 128)), *each(lambda r: (ZS, r, 128)),
            *each(lambda r: (r, 128), F32), *flats(), *flats(),
            D((2,)), D((LON,)), D((LON,)), D((20,)), D((20,)), D((16,)), D((GROUPS, XS)), D((16, XS)), D((16,)), D((GROUPS,)),
            D((3,)), D((3,)), D((3, XS, 2)), D((3, XS, 2)), D((3, ZS)), D((3, ZS)), D((3, 4)), D((3, 4)),
        ],
        compiler_params=pltpu.CompilerParams(collective_id=0, has_side_effects=True, vmem_limit_bytes=63 * 1024 * 1024),
        name="level",
    )(w1, w2, w3, x, c)


def finish_kernel(f, g, a, b, c, fo, go, ao, bo, co, fv, gv, av, bv, cv, isem, osem):
    trips = [(f, fv, fo), (a, av, ao), (b, bv, bo), (c, cv, co)]
    trips += [(g.at[16 * k : 16 * k + 16], gv.at[16 * k : 16 * k + 16], go.at[16 * k : 16 * k + 16]) for k in range(4)]
    ins = [pltpu.make_async_copy(src, mid, isem.at[i]) for i, (src, mid, _) in enumerate(trips)]
    outs = [pltpu.make_async_copy(mid, dst, osem.at[i]) for i, (_, mid, dst) in enumerate(trips)]
    for k in ins:
        k.start()
    for k, m in zip(ins, outs):
        k.wait()
        m.start()
    for m in outs:
        m.wait()


def finish(*arrays):
    hbm = pl.BlockSpec(memory_space=pl.ANY)
    return pl.pallas_call(
        finish_kernel,
        out_shape=tuple(jax.ShapeDtypeStruct(a.shape, a.dtype) for a in arrays),
        in_specs=[hbm] * 5,
        out_specs=(hbm,) * 5,
        scratch_shapes=[*[pltpu.VMEM(a.shape, a.dtype) for a in arrays],
                        pltpu.SemaphoreType.DMA((8,)), pltpu.SemaphoreType.DMA((8,))],
        name="results",
    )(*arrays)


def local(inputs, w_first, w_second, w_third, cotangent):
    return finish(*level(w_first, w_second, w_third, inputs, cotangent))


def solution(mesh):
    tile, flat = P("lat", "lon", None), P(("lat", "lon"))
    return jax.shard_map(
        local,
        mesh=mesh,
        in_specs=(tile, flat, flat, flat, tile),
        out_specs=(tile, tile, flat, flat, flat),
        check_vma=False,
    )
```

```python
import jax
import jax.numpy as jnp
from jax import lax
from jax.experimental import pallas as pl
from jax.experimental.pallas import tpu as pltpu
from jax.sharding import PartitionSpec as P

LOSS_CELLS = 1024
F32, BF16 = jnp.float32, jnp.bfloat16
W = 48
PITCH = 104
MESH = pl.DeviceIdType.MESH
LON, ZS, GROUPS = 8, 8, 32
S1, S2 = 864, 1296
XS = 4
ROWS = (14, 14, 9)
PACKED = (48, 48, 32)
ORDER = (4, 3, 5, 2, 6, 1, 7, 0)
STARTS = ((0, 13, 27, 40), (0, 13, 27, 40), (0, 9, 18, 27))


def mm(a, b):
    return lax.dot_general(a, b, (((1,), (0,)), ((), ())), preferred_element_type=F32)


def mmt(a, b):
    return lax.dot_general(a, b, (((1,), (1,)), ((), ())), preferred_element_type=F32)


def pieces(size, fold):
    out = []
    for row in range(size * LON // 192):
        at = row * 192
        while at < (row + 1) * 192:
            shard = at // size
            end = min((row + 1) * 192, (shard + 1) * size)
            out.append((shard, at - shard * size, row % fold, 192 * (row // fold) + at - row * 192, end - at))
            at = end
    return out


def group_map():
    moves = [(s, lane, 54 + row, at, n) for s, lane, row, at, n in pieces(S1, 18)]
    for k in range(2):
        moves += [(s, S1 + k * S2 + lane, row, 192 * k + at, n) for s, lane, row, at, n in pieces(S2, 54)]
    return moves


def flat_moves(size, shift, rows, y):
    out = []
    for piece in range(2):
        lane = 0
        while lane < size:
            at = shift + piece * size + lane
            row, col = at // 192, at % 192
            n = min(size - lane, (128 if col < 128 else 192) - col)
            spot = (y * rows + row, col) if col < 128 else (2 * rows + row, 64 * y + col - 128)
            out.append((piece, lane, *spot, n))
            lane += n
    return out


def place():
    lat, lon = lax.axis_index("lat"), lax.axis_index("lon")
    core = lax.rem(lat, 2)
    z = lax.rem(lax.div(lat, 2), ZS)
    yh = lax.div(lat, 2 * ZS)
    x = lax.div(lon, 2)
    yl = lax.rem(lon, 2)
    return lat, lon, yh, z, core, x, yl


def remote(src, dst, send, recv, peer):
    return pltpu.make_async_remote_copy(src_ref=src, dst_ref=dst, send_sem=send, recv_sem=recv,
                                        device_id=peer, device_id_type=MESH)


def level_kernel(w1, w2, w3, x_hbm, c_hbm, feat_ref, gin_ref, o1, o2, o3,
                 x_ref, c_ref, v_ref, vbuf, stage, own, eb, xe, xw, xn, xs, xne, xnw, xse, xsw,
                 ce, cw, cn, cs, cne, cnw, cse, csw, wb, tr,
                 xf, x0, x1, kf2, kf3, kg, k1, k2, k3, cf, hs1, hs2, ds3, ds2, bs, p2, dt, g1, g2, g3, st, il,
                 a3, a2, a1, r3, r2, r1, s3, s2, s1, q3, q2, q1, acc3, acc2, acc1, t3, t2, t1, z3, z2, z1,
                 u3, u2, u1, f3, f2, f1, l3, l2, l1,
                 isem, vsend, vrecv, hsend, hrecv, wsend, wrecv, fsend, psend, precv,
                 a_send, a_recv, x_send, x_recv, z_send, z_recv, y_send, y_recv):
    lat, lon, yh, z, core, x, yl = place()
    last = lax.axis_size("lat") - 1
    east, west = lax.rem(lon + 1, LON), lax.rem(lon + LON - 1, LON)
    north_of, south_of = lax.rem(lat + 31, 32), lax.rem(lat + 1, 32)
    partner = lat + 1 - 2 * core
    across = lax.rem(lat + 16, 32)
    beside = lon + 1 - 2 * yl
    lons = [lax.rem(lon + d, LON) for d in range(1, LON)]
    xq = [lax.rem(x + d, XS) for d in range(XS)]
    zs = [lax.rem(z + d, ZS) for d in range(ZS)]
    def lat_of(half, zz):
        return half * 16 + zz * 2 + core
    near = (1, 7, 2, 6, 3, 5, 4)
    lats = [lat_of(yh, zs[d]) for d in near] + [lat_of(1 - yh, zs[d]) for d in (0, *near)]

    ins = [pltpu.make_async_copy(x_hbm, x_ref, isem.at[0]), pltpu.make_async_copy(c_hbm, c_ref, isem.at[1])]
    for k in ins:
        k.start()
    v_ref[0:1, 0:S1] = w1[...].astype(F32).reshape(1, S1)
    v_ref[0:1, S1 : S1 + S2] = w2[...].astype(F32).reshape(1, S2)
    v_ref[0:1, S1 + S2 :] = w3[...].astype(F32).reshape(1, S2)
    sem = pltpu.get_barrier_semaphore()
    peers = [(lat, p) for p in lons] + [(q, lon) for q in (north_of, south_of, *lats)] + [(across, beside)]
    for peer in peers:
        pl.semaphore_signal(sem, inc=1, device_id=peer, device_id_type=MESH)
    pl.semaphore_wait(sem, len(peers))

    sends = []
    for d in range(1, LON):
        k = remote(v_ref, vbuf.at[lon], vsend.at[d], vrecv.at[lon], (lat, lons[d - 1]))
        k.start()
        sends.append(k)
    halos = []
    def halo(src, dst, peer):
        n = len(halos)
        k = remote(src, dst, hsend.at[n], hrecv.at[n], peer)
        k.start()
        halos.append(k)
        sends.append(k)
    e, w, n, s = (lat, east), (lat, west), (north_of, lon), (south_of, lon)
    halo(x_hbm.at[54:64], xn, s)
    halo(x_hbm.at[0:10], xs, n)
    ins[0].wait()
    for k in range(2):
        il[...] = x_ref[:, 48 * k : 48 * k + 16, :].astype(F32).reshape(1024, 128)
        for j in range(10):
            eb[k, j] = il[pl.ds(j + 6 * k, 64, stride=16), :].astype(BF16)
    halo(eb.at[0], xe, w)
    halo(eb.at[1], xw, e)
    ins[1].wait()

    vbuf[lon] = v_ref[...]
    for d in range(1, LON):
        src = lons[d - 1]
        remote(v_ref, vbuf.at[src], vsend.at[d], vrecv.at[src], (lat, src)).wait_recv()
    for shard, lane, row, at, length in group_map():
        stage[row : row + 1, at : at + length] = vbuf[shard, :, lane : lane + length]
    for t in range(3):
        tr[72 * t : 72 * t + 72, :] = stage[:, 128 * t : 128 * t + 128]
    tr[216:224, :] = jnp.zeros((8, 128), F32)
    for k in range(XS):
        own[k] = tr[56 * k : 56 * k + 56, :].astype(BF16)
    for i, q in enumerate(lats):
        k = remote(own.at[x], wb.at[lat, x], wsend.at[i], wrecv.at[lat, x], (q, lon))
        k.start()
        sends.append(k)
    k = remote(own, wb.at[lat], psend.at[15], precv.at[lat], (partner, lon))
    k.start()
    sends.append(k)
    wb[lat] = own[...]

    halo(c_ref.at[:, 0:8], ce, w)
    halo(c_ref.at[:, 24:32], cw, e)
    halo(c_ref.at[29:32], cn, s)
    halo(c_ref.at[0:3], cs, n)

    north = (lat > 0).astype(F32)
    south = (lat < last).astype(F32)
    def own_row(r, _):
        p = pl.multiple_of((r + 9) * PITCH, 8)
        xf[pl.ds(p + 8, 64), :] = x_ref[r].astype(F32)
        xf[pl.ds(p + 80, 16), :] = jnp.zeros((16, 128), F32)
        return 0
    lax.fori_loop(0, 64, own_row, 0)
    def forward(i):
        q = lats[i]
        remote(own.at[x], wb.at[q, x], wsend.at[i], wrecv.at[q, x], (q, lon)).wait_recv()
        for d in range(1, XS):
            k = remote(wb.at[q, x], wb.at[q, x], fsend.at[i, d], wrecv.at[q, x], (lat, xq[d] * 2 + yl))
            k.start()
            sends.append(k)
    def share(i):
        q = lats[i]
        for d in range(1, XS):
            remote(own.at[x], wb.at[q, xq[d]], fsend.at[i, d], wrecv.at[q, xq[d]], (lat, xq[d] * 2 + yl)).wait_recv()
        k = remote(wb.at[q], wb.at[q], psend.at[i], precv.at[q], (partner, lon))
        k.start()
        sends.append(k)
    for i in range(15):
        forward(i)
    halos[2].wait_recv()
    halos[3].wait_recv()
    halo(xe.at[:, 48:64], xne, s)
    halo(xw.at[:, 48:64], xnw, s)
    halo(xe.at[:, 0:16], xse, n)
    halo(xw.at[:, 0:16], xsw, n)
    sides = [(xe, xne, xse, (72 + j,), j) for j in range(10)] + [(xw, xnw, xsw, (94 + j, j - 2), j) for j in range(10)]
    for ref, rn, rs, ats, j in sides:
        for at in ats:
            if at >= 0:
                xf[pl.ds(9 * PITCH + at, 64, stride=PITCH), :] = ref[j].astype(F32)
    for i in range(5):
        share(i)
    def split(dst, p, idx):
        for k in range(3):
            dst[idx, :, 128 * k : 128 * k + 128] = xf[pl.ds(p * PITCH + 7 + k, W, stride=2), :].astype(BF16)
    def split_pair(k, _):
        split(x0, 2 * k, k)
        split(x1, 2 * k + 1, k)
        return 0
    lax.fori_loop(5, 36, split_pair, 0)
    for i in range(5, 10):
        share(i)
    for k in (0, 1, 8, 9, 10, 11):
        halos[k].wait_recv()
    for q in range(9):
        xf[q * PITCH + 8 : q * PITCH + 72, :] = xn[q + 1].astype(F32) * north
        xf[q * PITCH + 80 : q * PITCH + 96, :] = jnp.zeros((16, 128), F32)
    for q in range(10):
        xf[(q + 73) * PITCH + 8 : (q + 73) * PITCH + 72, :] = xs[q].astype(F32) * south
        xf[(q + 73) * PITCH + 80 : (q + 73) * PITCH + 96, :] = jnp.zeros((16, 128), F32)
    for ref, rn, rs, ats, j in sides:
        top = rn[j].astype(F32)[7:16] * north
        low = rs[j].astype(F32)[0:10] * south
        for at in ats:
            if at >= 0:
                xf[pl.ds(at, 9, stride=PITCH), :] = top
                xf[pl.ds(73 * PITCH + at, 10, stride=PITCH), :] = low
    for i in range(10, 15):
        share(i)
    lax.fori_loop(0, 5, split_pair, 0)
    lax.fori_loop(36, 41, split_pair, 0)
    split(x0, 82, 41)
    for half in range(2):
        for zz in range(ZS):
            q = half * 16 + zz * 2 + 1 - core
            remote(own, wb.at[q], psend.at[15], precv.at[q], (partner, lon)).wait_recv()

    for g in range(GROUPS):
        for k in range(XS):
            tr[56 * k : 56 * k + 56, :] = wb[g, k].astype(F32)
        at = 54 * g
        kf2[at : at + 54, 0:128] = tr[0:54, :]
        kf2[at : at + 54, 128:192] = tr[72:126, 0:64]
        kf3[at : at + 54, 0:64] = tr[72:126, 64:128]
        kf3[at : at + 54, 64:192] = tr[144:198, :]
        at = 36 * g
        kg[at : at + 18, 0:128] = tr[54:72, :]
        kg[at : at + 18, 128:192] = tr[126:144, 0:64]
        kg[at + 18 : at + 36, 0:64] = tr[126:144, 64:128]
        kg[at + 18 : at + 36, 64:192] = tr[198:216, :]
    k1[...] = kg[...].astype(BF16)
    k2[...] = kf2[...].astype(BF16)
    k3[...] = kf3[...].astype(BF16)

    def rows_ok(start, n, first):
        i = lax.broadcasted_iota(jnp.int32, (n, W, 192), 0) + (start + first)
        glob = i + 32 * lat
        return (glob >= 0) & (glob < 32 * (last + 1))
    def put_shifted(dst, start, n, value):
        dst[1, pl.ds(start, n)] = value.astype(BF16)
        dst[0, pl.ds(start, n)] = pltpu.roll(value, 1, 1).astype(BF16)
        dst[2, pl.ds(start, n)] = pltpu.roll(value, W - 1, 1).astype(BF16)
    def chunks(total, n, body, lo=0, hi=None):
        count = -(-total // n)
        def step(k, _):
            body(jnp.minimum(k * n, total - n))
            return 0
        lax.fori_loop(lo, count if hi is None else hi, step, 0)

    def h_one(s):
        n = 14
        acc = mm(x0[pl.ds(s, n)].reshape(n * W, 384), k1[0:384])
        acc += mm(x1[pl.ds(s, n)].reshape(n * W, 384), k1[384:768])
        acc += mm(x0[pl.ds(s + 1, n)].reshape(n * W, 384), k1[768:1152])
        put_shifted(hs1, s, n, jnp.where(rows_ok(s, n, -4), acc.reshape(n, W, 192), 0.0))
    chunks(41, 14, h_one)

    halos[4].wait_recv()
    halos[5].wait_recv()
    halo(ce.at[29:32], cne, s)
    halo(cw.at[29:32], cnw, s)
    halo(ce.at[0:3], cse, n)
    halo(cw.at[0:3], csw, n)

    def conv(src, k, s, n):
        acc = None
        for a in range(3):
            for b in range(3):
                t = mm(src[b, pl.ds(s + a, n)].reshape(n * W, 192), k[(3 * a + b) * 192 : (3 * a + b + 1) * 192])
                acc = t if acc is None else acc + t
        return acc.reshape(n, W, 192)
    def tconv(src, k, s, n):
        acc = None
        for a in range(3):
            for b in range(3):
                t = mmt(src[2 - b, pl.ds(s + 2 - a, n)].reshape(n * W, 192), k[(3 * a + b) * 192 : (3 * a + b + 1) * 192])
                acc = t if acc is None else acc + t
        return acc.reshape(n, W, 192)

    def h_two(s):
        n = 13
        v = conv(hs1, k2, s, n)
        p2[pl.ds(s, n)] = v
        h = v / (1.0 + jnp.exp(-v))
        put_shifted(hs2, s, n, jnp.where(rows_ok(s, n, -3), h, 0.0))
    chunks(39, 13, h_two)

    for k in halos[6:8] + halos[12:16]:
        k.wait_recv()
    def cot(idx, row, e, w):
        cf[idx, 0:32, :] = row.astype(F32)
        cf[idx, 32:40, :] = e.astype(F32)
        cf[idx, 40:48, :] = w.astype(F32)
    def cot_own(k, _):
        cot(k + 2, c_ref[k], ce[k], cw[k])
        return 0
    lax.fori_loop(0, 32, cot_own, 0)
    for q in range(2):
        cot(q, cn[q + 1], cne[q + 1], cnw[q + 1])
    for q in range(3):
        cot(q + 34, cs[q], cse[q], csw[q])

    def deriv(v):
        sg = 1.0 / (1.0 + jnp.exp(-v))
        return sg, sg * (1.0 + v * (1.0 - sg))
    def d_three(s):
        n = 13
        v = conv(hs2, k3, s, n)
        sg, dv = deriv(v)
        bs[1, pl.ds(s, n)] = (v * sg).astype(BF16)
        put_shifted(ds3, s, n, jnp.where(rows_ok(s, n, -2), cf[pl.ds(s, n)] * dv, 0.0))
    chunks(37, 13, d_three)
    feat_ref[...] = bs[1, 2:34, 0:32, :]

    def wgrad(src, off, dst):
        for a in range(3):
            for b in range(3):
                win = src[b, off + a : off + a + 32, 0:32, :].reshape(1024, 192)
                t = mm(dt[...], win)
                n0 = (3 * a + b) * 192
                dst[n0 : n0 + 192, :] = t.T
    st[...] = jnp.zeros_like(st)
    def to_partner(i, g, a, r):
        rows, group = ROWS[i], 36 if i == 2 else 54
        for zz in range(ZS):
            for c in range(2):
                for q in range(XS):
                    for y in range(2):
                        base = (y * 16 + zz * 2 + c) * group + STARTS[i][q]
                        st[y * rows : (y + 1) * rows, :] = g[base : base + rows, 0:128]
                        st[2 * rows : 3 * rows, 64 * y : 64 * y + 64] = g[base : base + rows, 128:192]
                    a[zz, c, q] = st[0 : PACKED[i], :].astype(BF16)
        k = remote(a.at[:, 1 - core], r, a_send.at[i], a_recv.at[i], (partner, lon))
        k.start()
        sends.append(k)
        return k
    def along_x(i, k, a, r, sx, qx, acc):
        k.wait_recv()
        for half in range(2):
            for d in (2, 1, 3, 0):
                q = xq[d]
                for p in range(4 * half, 4 * half + 4):
                    zz = zs[ORDER[p]]
                    total = a[zz, core, q].astype(F32) + r[zz, q].astype(F32)
                    if d:
                        sx[d, p] = total.astype(BF16)
                    else:
                        acc[p] = total
                if d:
                    part = pl.ds(4 * half, 4)
                    m = remote(sx.at[d, part], qx.at[x, part], x_send.at[i, d, half], x_recv.at[i, x, half], (lat, q * 2 + yl))
                    m.start()
                    sends.append(m)
    def along_z(i, sx, qx, acc, tz, zb):
        for half in range(2):
            part = pl.ds(4 * half, 4)
            for d in (1, 3, 2):
                q = xq[d]
                remote(sx.at[d, part], qx.at[q, part], x_send.at[i, d, half], x_recv.at[i, q, half], (lat, q * 2 + yl)).wait_recv()
            for p in range(4 * half, 4 * half + 4):
                d = ORDER[p]
                total = acc[p] + (qx[xq[1], p].astype(F32) + qx[xq[3], p].astype(F32)) + qx[xq[2], p].astype(F32)
                if d:
                    tz[d] = total.astype(BF16)
                    m = remote(tz.at[d], zb.at[z], z_send.at[i, d], z_recv.at[i, z], (lat_of(yh, zs[d]), lon))
                    m.start()
                    sends.append(m)
                else:
                    acc[p] = total
    ys = [(1 - yh, yl, (across, lon)), (yh, 1 - yl, (lat, beside)), (1 - yh, 1 - yl, (across, beside))]
    def along_y(i, acc, tz, zb, u, f, l):
        size = S1 if i == 2 else S2
        total = acc[7]
        for d in near:
            zz = zs[d]
            remote(tz.at[d], zb.at[zz], z_send.at[i, d], z_recv.at[i, zz], (lat_of(yh, zz), lon)).wait_recv()
            total = total + zb[zz].astype(F32)
        u[...] = total
        def cut(shift):
            for y in range(2):
                for piece, lane, row, at, length in flat_moves(size, shift, ROWS[i], y):
                    f[2 * y + piece, :, lane : lane + length] = u[row : row + 1, at : at + length]
        if i == 2:
            cut(0)
        else:
            @pl.when(lax.rem(x, 2) == 0)
            def _():
                cut(0)
            @pl.when(lax.rem(x, 2) == 1)
            def _():
                cut(96)
        me = 2 * yh + yl
        for d, (h, b, peer) in enumerate(ys):
            m = remote(f.at[2 * h + b], l.at[me], y_send.at[i, d], y_recv.at[i, me], peer)
            m.start()
            sends.append(m)
        l[me] = f[me]
    def total_of(i, f, l):
        for d, (h, b, peer) in enumerate(ys):
            remote(f.at[2 * h + b], l.at[2 * h + b], y_send.at[i, d], y_recv.at[i, 2 * h + b], peer).wait_recv()
        return (((l[0] + l[1]) + (l[2] + l[3])) * (1.0 / LOSS_CELLS)).reshape(S1 if i == 2 else S2)

    dt[...] = ds3[1, 2:34, 0:32, :].reshape(1024, 192).T
    wgrad(hs2, 2, g3)
    c3 = to_partner(0, g3, a3, r3)

    def d_two(s):
        n = 12
        v = tconv(ds3, k3, s, n)
        _, dv = deriv(p2[pl.ds(s + 2, n)])
        put_shifted(ds2, s, n, jnp.where(rows_ok(s, n, -1), v * dv, 0.0))
    chunks(35, 12, d_two)
    along_x(0, c3, a3, r3, s3, q3, acc3)
    dt[...] = ds2[1, 1:33, 0:32, :].reshape(1024, 192).T
    wgrad(hs1, 3, g2)
    c2 = to_partner(1, g2, a2, r2)

    def b_one(s):
        n = 11
        v = jnp.where(rows_ok(s, n, 0), tconv(ds2, k2, s, n), 0.0)
        bs[1, pl.ds(s, n)] = v.astype(BF16)
        bs[2, pl.ds(s, n)] = pltpu.roll(v, W - 1, 1).astype(BF16)
    chunks(33, 11, b_one, 0, 1)
    along_x(1, c2, a2, r2, s2, q2, acc2)
    chunks(33, 11, b_one, 1, 2)
    along_z(0, s3, q3, acc3, t3, z3)
    chunks(33, 11, b_one, 2, 3)
    dt[...] = bs[1, 0:32, 0:32, :].reshape(1024, 192).T
    for a in range(3):
        src = x1 if a == 1 else x0
        off = 4 + (a == 2)
        win = src[off : off + 32, 0:32, :].reshape(1024, 384)
        g1[384 * a : 384 * a + 384, :] = mm(dt[...], win).T
    c1 = to_partner(2, g1, a1, r1)
    along_z(1, s2, q2, acc2, t2, z2)
    def k1t(a, b):
        n0 = (3 * a + b) * 128
        return k1[n0 : n0 + 128]
    def gin(i):
        n = 8
        here = bs[1, pl.ds(i, n), 0:32, :].reshape(n * 32, 192)
        right = bs[2, pl.ds(i, n), 0:32, :].reshape(n * 32, 192)
        below = bs[1, pl.ds(i + 1, n), 0:32, :].reshape(n * 32, 192)
        corner = bs[2, pl.ds(i + 1, n), 0:32, :].reshape(n * 32, 192)
        ee = mmt(here, k1t(1, 1))
        eo = mmt(right, k1t(1, 0)) + mmt(here, k1t(1, 2))
        oe = mmt(below, k1t(0, 1)) + mmt(here, k1t(2, 1))
        oo = mmt(corner, k1t(0, 0)) + mmt(below, k1t(0, 2)) + mmt(right, k1t(2, 0)) + mmt(here, k1t(2, 2))
        il[pl.ds(0, n * 32, stride=2), :] = ee
        il[pl.ds(1, n * 32, stride=2), :] = eo
        il[pl.ds(n * 64, n * 32, stride=2), :] = oe
        il[pl.ds(n * 64 + 1, n * 32, stride=2), :] = oo
        even = il[0 : n * 64, :].reshape(n, 64, 128).astype(BF16)
        odd = il[n * 64 : n * 128, :].reshape(n, 64, 128).astype(BF16)
        for m in range(n):
            gin_ref[2 * (i + m)] = even[m]
            gin_ref[2 * (i + m) + 1] = odd[m]
    chunks(32, 8, gin, 0, 1)
    along_x(2, c1, a1, r1, s1, q1, acc1)
    chunks(32, 8, gin, 1, 4)
    along_z(2, s1, q1, acc1, t1, z1)
    along_y(0, acc3, t3, z3, u3, f3, l3)
    along_y(1, acc2, t2, z2, u2, f2, l2)
    o3[...] = total_of(0, f3, l3)
    o2[...] = total_of(1, f2, l2)
    along_y(2, acc1, t1, z1, u1, f1, l1)
    o1[...] = total_of(2, f1, l1)
    for k in sends:
        k.wait_send()


def level(w1, w2, w3, x, c):
    V, D = pltpu.VMEM, pltpu.SemaphoreType.DMA
    vm = pl.BlockSpec(memory_space=pltpu.VMEM)
    hbm = pl.BlockSpec(memory_space=pl.ANY)
    sds = jax.ShapeDtypeStruct
    def each(shape_of, dtype=BF16):
        return [V(shape_of(r), dtype) for r in PACKED]
    def flats():
        return [V((4, 1, n), F32) for n in (S2, S2, S1)]
    halos = [(10, 64, 128)] * 4 + [(10, 16, 128)] * 4 + [(32, 8, 192)] * 2 + [(3, 32, 192)] * 2 + [(3, 8, 192)] * 4
    return pl.pallas_call(
        level_kernel,
        out_shape=(sds((32, 32, 192), BF16), sds((64, 64, 128), BF16), sds((S1,), F32), sds((S2,), F32), sds((S2,), F32)),
        in_specs=[vm, vm, vm, hbm, hbm],
        out_specs=(vm,) * 5,
        scratch_shapes=[
            V((64, 64, 128), BF16), V((32, 32, 192), BF16), V((1, 3456), F32), V((LON, 1, 3456), F32), V((72, 384), F32),
            V((XS, 56, 128), BF16), V((2, 10, 64, 128), BF16), *[V(s, BF16) for s in halos],
            V((GROUPS, XS, 56, 128), BF16), V((224, 128), F32),
            V((90 * PITCH, 128), F32), V((42, W, 384), BF16), V((42, W, 384), BF16),
            V((1728, 192), F32), V((1728, 192), F32), V((1152, 192), F32),
            V((1152, 192), BF16), V((1728, 192), BF16), V((1728, 192), BF16),
            V((37, W, 192), F32), V((3, 41, W, 192), BF16), V((3, 39, W, 192), BF16),
            V((3, 37, W, 192), BF16), V((3, 35, W, 192), BF16), V((3, 37, W, 192), BF16),
            V((39, W, 192), F32), V((192, 1024), BF16), V((1152, 192), F32), V((1728, 192), F32), V((1728, 192), F32),
            V((48, 128), F32), V((1024, 128), F32),
            *each(lambda r: (ZS, 2, XS, r, 128)), *each(lambda r: (ZS, XS, r, 128)),
            *each(lambda r: (XS, ZS, r, 128)), *each(lambda r: (XS, ZS, r, 128)),
            *each(lambda r: (ZS, r, 128), F32), *each(lambda r: (ZS, r, 128)), *each(lambda r: (ZS, r, 128)),
            *each(lambda r: (r, 128), F32), *flats(), *flats(),
            D((2,)), D((LON,)), D((LON,)), D((20,)), D((20,)), D((16,)), D((GROUPS, XS)), D((16, XS)), D((16,)), D((GROUPS,)),
            D((3,)), D((3,)), D((3, XS, 2)), D((3, XS, 2)), D((3, ZS)), D((3, ZS)), D((3, 4)), D((3, 4)),
        ],
        compiler_params=pltpu.CompilerParams(collective_id=0, has_side_effects=True, vmem_limit_bytes=63 * 1024 * 1024),
        name="level",
    )(w1, w2, w3, x, c)


def finish_kernel(f, g, a, b, c, fo, go, ao, bo, co, fv, gv, av, bv, cv, isem, osem):
    trips = [(f, fv, fo), (a, av, ao), (b, bv, bo), (c, cv, co)]
    trips += [(g.at[16 * k : 16 * k + 16], gv.at[16 * k : 16 * k + 16], go.at[16 * k : 16 * k + 16]) for k in range(4)]
    ins = [pltpu.make_async_copy(src, mid, isem.at[i]) for i, (src, mid, _) in enumerate(trips)]
    outs = [pltpu.make_async_copy(mid, dst, osem.at[i]) for i, (_, mid, dst) in enumerate(trips)]
    for k in ins:
        k.start()
    for k, m in zip(ins, outs):
        k.wait()
        m.start()
    for m in outs:
        m.wait()


def finish(*arrays):
    hbm = pl.BlockSpec(memory_space=pl.ANY)
    return pl.pallas_call(
        finish_kernel,
        out_shape=tuple(jax.ShapeDtypeStruct(a.shape, a.dtype) for a in arrays),
        in_specs=[hbm] * 5,
        out_specs=(hbm,) * 5,
        scratch_shapes=[*[pltpu.VMEM(a.shape, a.dtype) for a in arrays],
                        pltpu.SemaphoreType.DMA((8,)), pltpu.SemaphoreType.DMA((8,))],
        name="results",
    )(*arrays)


def local(inputs, w_first, w_second, w_third, cotangent):
    return finish(*level(w_first, w_second, w_third, inputs, cotangent))


def solution(mesh):
    tile, flat = P("lat", "lon", None), P(("lat", "lon"))
    return jax.shard_map(
        local,
        mesh=mesh,
        in_specs=(tile, flat, flat, flat, tile),
        out_specs=(tile, tile, flat, flat, flat),
        check_vma=False,
    )
```

```python
import jax
import jax.numpy as jnp
from jax import lax
from jax.experimental import pallas as pl
from jax.experimental.pallas import tpu as pltpu
from jax.sharding import PartitionSpec as P

LOSS_CELLS = 1024
F32, BF16 = jnp.float32, jnp.bfloat16
W = 48
PITCH = 104
MESH = pl.DeviceIdType.MESH
LON, ZS, GROUPS = 8, 8, 32
S1, S2 = 864, 1296
XS = 4
ROWS = (14, 14, 9)
PACKED = (48, 48, 32)
ORDER = (4, 3, 5, 2, 6, 1, 7, 0)
STARTS = ((0, 13, 27, 40), (0, 13, 27, 40), (0, 9, 18, 27))


def mm(a, b):
    return lax.dot_general(a, b, (((1,), (0,)), ((), ())), preferred_element_type=F32)


def mmt(a, b):
    return lax.dot_general(a, b, (((1,), (1,)), ((), ())), preferred_element_type=F32)


def pieces(size, fold):
    out = []
    for row in range(size * LON // 192):
        at = row * 192
        while at < (row + 1) * 192:
            shard = at // size
            end = min((row + 1) * 192, (shard + 1) * size)
            out.append((shard, at - shard * size, row % fold, 192 * (row // fold) + at - row * 192, end - at))
            at = end
    return out


def group_map():
    moves = [(s, lane, 54 + row, at, n) for s, lane, row, at, n in pieces(S1, 18)]
    for k in range(2):
        moves += [(s, S1 + k * S2 + lane, row, 192 * k + at, n) for s, lane, row, at, n in pieces(S2, 54)]
    return moves


def flat_moves(size, shift, rows, y):
    out = []
    for piece in range(2):
        lane = 0
        while lane < size:
            at = shift + piece * size + lane
            row, col = at // 192, at % 192
            n = min(size - lane, (128 if col < 128 else 192) - col)
            spot = (y * rows + row, col) if col < 128 else (2 * rows + row, 64 * y + col - 128)
            out.append((piece, lane, *spot, n))
            lane += n
    return out


def place():
    lat, lon = lax.axis_index("lat"), lax.axis_index("lon")
    core = lax.rem(lat, 2)
    z = lax.rem(lax.div(lat, 2), ZS)
    yh = lax.div(lat, 2 * ZS)
    x = lax.div(lon, 2)
    yl = lax.rem(lon, 2)
    return lat, lon, yh, z, core, x, yl


def remote(src, dst, send, recv, peer):
    return pltpu.make_async_remote_copy(src_ref=src, dst_ref=dst, send_sem=send, recv_sem=recv,
                                        device_id=peer, device_id_type=MESH)


def level_kernel(w1, w2, w3, x_hbm, c_hbm, feat_ref, gin_ref, o1, o2, o3,
                 x_ref, c_ref, v_ref, vbuf, stage, own, eb, xe, xw, xn, xs, xne, xnw, xse, xsw,
                 ce, cw, cn, cs, cne, cnw, cse, csw, wb, tr,
                 xf, x0, x1, kf2, kf3, kg, k1, k2, k3, cf, hs1, hs2, ds3, ds2, bs, p2, dt, g1, g2, g3, st, il,
                 a3, a2, a1, r3, r2, r1, s3, s2, s1, q3, q2, q1, acc3, acc2, acc1, t3, t2, t1, z3, z2, z1,
                 u3, u2, u1, f3, f2, f1, l3, l2, l1,
                 isem, vsend, vrecv, hsend, hrecv, wsend, wrecv, fsend, psend, precv,
                 a_send, a_recv, x_send, x_recv, z_send, z_recv, y_send, y_recv):
    lat, lon, yh, z, core, x, yl = place()
    last = lax.axis_size("lat") - 1
    east, west = lax.rem(lon + 1, LON), lax.rem(lon + LON - 1, LON)
    north_of, south_of = lax.rem(lat + 31, 32), lax.rem(lat + 1, 32)
    partner = lat + 1 - 2 * core
    across = lax.rem(lat + 16, 32)
    beside = lon + 1 - 2 * yl
    lons = [lax.rem(lon + d, LON) for d in range(1, LON)]
    xq = [lax.rem(x + d, XS) for d in range(XS)]
    zs = [lax.rem(z + d, ZS) for d in range(ZS)]
    def lat_of(half, zz):
        return half * 16 + zz * 2 + core
    near = (1, 7, 2, 6, 3, 5, 4)
    lats = [lat_of(yh, zs[d]) for d in near] + [lat_of(1 - yh, zs[d]) for d in (0, *near)]

    ins = [pltpu.make_async_copy(x_hbm, x_ref, isem.at[0]), pltpu.make_async_copy(c_hbm, c_ref, isem.at[1])]
    for k in ins:
        k.start()
    v_ref[0:1, 0:S1] = w1[...].astype(F32).reshape(1, S1)
    v_ref[0:1, S1 : S1 + S2] = w2[...].astype(F32).reshape(1, S2)
    v_ref[0:1, S1 + S2 :] = w3[...].astype(F32).reshape(1, S2)
    sem = pltpu.get_barrier_semaphore()
    peers = [(lat, p) for p in lons] + [(q, lon) for q in (north_of, south_of, *lats)] + [(across, beside)]
    for peer in peers:
        pl.semaphore_signal(sem, inc=1, device_id=peer, device_id_type=MESH)
    pl.semaphore_wait(sem, len(peers))

    sends = []
    for d in range(1, LON):
        k = remote(v_ref, vbuf.at[lon], vsend.at[d], vrecv.at[lon], (lat, lons[d - 1]))
        k.start()
        sends.append(k)
    halos = []
    def halo(src, dst, peer):
        n = len(halos)
        k = remote(src, dst, hsend.at[n], hrecv.at[n], peer)
        k.start()
        halos.append(k)
        sends.append(k)
    e, w, n, s = (lat, east), (lat, west), (north_of, lon), (south_of, lon)
    halo(x_hbm.at[54:64], xn, s)
    halo(x_hbm.at[0:10], xs, n)
    ins[0].wait()
    for k in range(2):
        il[...] = x_ref[:, 48 * k : 48 * k + 16, :].astype(F32).reshape(1024, 128)
        for j in range(10):
            eb[k, j] = il[pl.ds(j + 6 * k, 64, stride=16), :].astype(BF16)
    halo(eb.at[0], xe, w)
    halo(eb.at[1], xw, e)
    ins[1].wait()

    vbuf[lon] = v_ref[...]
    for d in range(1, LON):
        src = lons[d - 1]
        remote(v_ref, vbuf.at[src], vsend.at[d], vrecv.at[src], (lat, src)).wait_recv()
    for shard, lane, row, at, length in group_map():
        stage[row : row + 1, at : at + length] = vbuf[shard, :, lane : lane + length]
    for t in range(3):
        tr[72 * t : 72 * t + 72, :] = stage[:, 128 * t : 128 * t + 128]
    tr[216:224, :] = jnp.zeros((8, 128), F32)
    for k in range(XS):
        own[k] = tr[56 * k : 56 * k + 56, :].astype(BF16)
    for i, q in enumerate(lats):
        k = remote(own.at[x], wb.at[lat, x], wsend.at[i], wrecv.at[lat, x], (q, lon))
        k.start()
        sends.append(k)
    k = remote(own, wb.at[lat], psend.at[15], precv.at[lat], (partner, lon))
    k.start()
    sends.append(k)
    wb[lat] = own[...]


    north = (lat > 0).astype(F32)
    south = (lat < last).astype(F32)
    def own_row(r, _):
        p = pl.multiple_of((r + 9) * PITCH, 8)
        xf[pl.ds(p + 8, 64), :] = x_ref[r].astype(F32)
        xf[pl.ds(p + 80, 16), :] = jnp.zeros((16, 128), F32)
        return 0
    lax.fori_loop(0, 64, own_row, 0)
    def forward(i):
        q = lats[i]
        remote(own.at[x], wb.at[q, x], wsend.at[i], wrecv.at[q, x], (q, lon)).wait_recv()
        for d in range(1, XS):
            k = remote(wb.at[q, x], wb.at[q, x], fsend.at[i, d], wrecv.at[q, x], (lat, xq[d] * 2 + yl))
            k.start()
            sends.append(k)
    def share(i):
        q = lats[i]
        for d in range(1, XS):
            remote(own.at[x], wb.at[q, xq[d]], fsend.at[i, d], wrecv.at[q, xq[d]], (lat, xq[d] * 2 + yl)).wait_recv()
        k = remote(wb.at[q], wb.at[q], psend.at[i], precv.at[q], (partner, lon))
        k.start()
        sends.append(k)
    for i in range(15):
        forward(i)
    halos[2].wait_recv()
    halos[3].wait_recv()
    halo(xe.at[:, 48:64], xne, s)
    halo(xw.at[:, 48:64], xnw, s)
    halo(xe.at[:, 0:16], xse, n)
    halo(xw.at[:, 0:16], xsw, n)
    sides = [(xe, xne, xse, (72 + j,), j) for j in range(10)] + [(xw, xnw, xsw, (94 + j, j - 2), j) for j in range(10)]
    for ref, rn, rs, ats, j in sides:
        for at in ats:
            if at >= 0:
                xf[pl.ds(9 * PITCH + at, 64, stride=PITCH), :] = ref[j].astype(F32)
    for i in range(5):
        share(i)
    def split(dst, p, idx):
        for k in range(3):
            dst[idx, :, 128 * k : 128 * k + 128] = xf[pl.ds(p * PITCH + 7 + k, W, stride=2), :].astype(BF16)
    def split_pair(k, _):
        split(x0, 2 * k, k)
        split(x1, 2 * k + 1, k)
        return 0
    lax.fori_loop(5, 36, split_pair, 0)
    for i in range(5, 10):
        share(i)
    for k in (0, 1, 4, 5, 6, 7):
        halos[k].wait_recv()
    for q in range(9):
        xf[q * PITCH + 8 : q * PITCH + 72, :] = xn[q + 1].astype(F32) * north
        xf[q * PITCH + 80 : q * PITCH + 96, :] = jnp.zeros((16, 128), F32)
    for q in range(10):
        xf[(q + 73) * PITCH + 8 : (q + 73) * PITCH + 72, :] = xs[q].astype(F32) * south
        xf[(q + 73) * PITCH + 80 : (q + 73) * PITCH + 96, :] = jnp.zeros((16, 128), F32)
    for ref, rn, rs, ats, j in sides:
        top = rn[j].astype(F32)[7:16] * north
        low = rs[j].astype(F32)[0:10] * south
        for at in ats:
            if at >= 0:
                xf[pl.ds(at, 9, stride=PITCH), :] = top
                xf[pl.ds(73 * PITCH + at, 10, stride=PITCH), :] = low
    for i in range(10, 15):
        share(i)
    halo(c_ref.at[:, 0:8], ce, w)
    halo(c_ref.at[:, 24:32], cw, e)
    halo(c_ref.at[29:32], cn, s)
    halo(c_ref.at[0:3], cs, n)
    lax.fori_loop(0, 5, split_pair, 0)
    lax.fori_loop(36, 41, split_pair, 0)
    split(x0, 82, 41)
    for half in range(2):
        for zz in range(ZS):
            q = half * 16 + zz * 2 + 1 - core
            remote(own, wb.at[q], psend.at[15], precv.at[q], (partner, lon)).wait_recv()

    for g in range(GROUPS):
        for k in range(XS):
            tr[56 * k : 56 * k + 56, :] = wb[g, k].astype(F32)
        at = 54 * g
        kf2[at : at + 54, 0:128] = tr[0:54, :]
        kf2[at : at + 54, 128:192] = tr[72:126, 0:64]
        kf3[at : at + 54, 0:64] = tr[72:126, 64:128]
        kf3[at : at + 54, 64:192] = tr[144:198, :]
        at = 36 * g
        kg[at : at + 18, 0:128] = tr[54:72, :]
        kg[at : at + 18, 128:192] = tr[126:144, 0:64]
        kg[at + 18 : at + 36, 0:64] = tr[126:144, 64:128]
        kg[at + 18 : at + 36, 64:192] = tr[198:216, :]
    k1[...] = kg[...].astype(BF16)
    k2[...] = kf2[...].astype(BF16)
    k3[...] = kf3[...].astype(BF16)

    def rows_ok(start, n, first):
        i = lax.broadcasted_iota(jnp.int32, (n, W, 192), 0) + (start + first)
        glob = i + 32 * lat
        return (glob >= 0) & (glob < 32 * (last + 1))
    def put_shifted(dst, start, n, value):
        dst[1, pl.ds(start, n)] = value.astype(BF16)
        dst[0, pl.ds(start, n)] = pltpu.roll(value, 1, 1).astype(BF16)
        dst[2, pl.ds(start, n)] = pltpu.roll(value, W - 1, 1).astype(BF16)
    def chunks(total, n, body, lo=0, hi=None):
        count = -(-total // n)
        def step(k, _):
            body(jnp.minimum(k * n, total - n))
            return 0
        lax.fori_loop(lo, count if hi is None else hi, step, 0)

    def h_one(s):
        n = 14
        acc = mm(x0[pl.ds(s, n)].reshape(n * W, 384), k1[0:384])
        acc += mm(x1[pl.ds(s, n)].reshape(n * W, 384), k1[384:768])
        acc += mm(x0[pl.ds(s + 1, n)].reshape(n * W, 384), k1[768:1152])
        put_shifted(hs1, s, n, jnp.where(rows_ok(s, n, -4), acc.reshape(n, W, 192), 0.0))
    chunks(41, 14, h_one)

    def conv(src, k, s, n):
        acc = None
        for a in range(3):
            for b in range(3):
                t = mm(src[b, pl.ds(s + a, n)].reshape(n * W, 192), k[(3 * a + b) * 192 : (3 * a + b + 1) * 192])
                acc = t if acc is None else acc + t
        return acc.reshape(n, W, 192)
    def tconv(src, k, s, n):
        acc = None
        for a in range(3):
            for b in range(3):
                t = mmt(src[2 - b, pl.ds(s + 2 - a, n)].reshape(n * W, 192), k[(3 * a + b) * 192 : (3 * a + b + 1) * 192])
                acc = t if acc is None else acc + t
        return acc.reshape(n, W, 192)

    def h_two(s):
        n = 13
        v = conv(hs1, k2, s, n)
        p2[pl.ds(s, n)] = v
        h = v / (1.0 + jnp.exp(-v))
        put_shifted(hs2, s, n, jnp.where(rows_ok(s, n, -3), h, 0.0))
    chunks(39, 13, h_two, 0, 2)
    halos[8].wait_recv()
    halos[9].wait_recv()
    halo(ce.at[29:32], cne, s)
    halo(cw.at[29:32], cnw, s)
    halo(ce.at[0:3], cse, n)
    halo(cw.at[0:3], csw, n)
    chunks(39, 13, h_two, 2, 3)

    for k in halos[10:16]:
        k.wait_recv()
    def cot(idx, row, e, w):
        cf[idx, 0:32, :] = row.astype(F32)
        cf[idx, 32:40, :] = e.astype(F32)
        cf[idx, 40:48, :] = w.astype(F32)
    def cot_own(k, _):
        cot(k + 2, c_ref[k], ce[k], cw[k])
        return 0
    lax.fori_loop(0, 32, cot_own, 0)
    for q in range(2):
        cot(q, cn[q + 1], cne[q + 1], cnw[q + 1])
    for q in range(3):
        cot(q + 34, cs[q], cse[q], csw[q])

    def deriv(v):
        sg = 1.0 / (1.0 + jnp.exp(-v))
        return sg, sg * (1.0 + v * (1.0 - sg))
    def d_three(s):
        n = 13
        v = conv(hs2, k3, s, n)
        sg, dv = deriv(v)
        bs[1, pl.ds(s, n)] = (v * sg).astype(BF16)
        put_shifted(ds3, s, n, jnp.where(rows_ok(s, n, -2), cf[pl.ds(s, n)] * dv, 0.0))
    chunks(37, 13, d_three)
    feat_ref[...] = bs[1, 2:34, 0:32, :]

    def wgrad(src, off, dst):
        for a in range(3):
            for b in range(3):
                win = src[b, off + a : off + a + 32, 0:32, :].reshape(1024, 192)
                t = mm(dt[...], win)
                n0 = (3 * a + b) * 192
                dst[n0 : n0 + 192, :] = t.T
    st[...] = jnp.zeros_like(st)
    def to_partner(i, g, a, r):
        rows, group = ROWS[i], 36 if i == 2 else 54
        for zz in range(ZS):
            for c in range(2):
                for q in range(XS):
                    for y in range(2):
                        base = (y * 16 + zz * 2 + c) * group + STARTS[i][q]
                        st[y * rows : (y + 1) * rows, :] = g[base : base + rows, 0:128]
                        st[2 * rows : 3 * rows, 64 * y : 64 * y + 64] = g[base : base + rows, 128:192]
                    a[zz, c, q] = st[0 : PACKED[i], :].astype(BF16)
        k = remote(a.at[:, 1 - core], r, a_send.at[i], a_recv.at[i], (partner, lon))
        k.start()
        sends.append(k)
        return k
    def along_x(i, k, a, r, sx, qx, acc):
        k.wait_recv()
        for half in range(2):
            for d in (2, 1, 3, 0):
                q = xq[d]
                for p in range(4 * half, 4 * half + 4):
                    zz = zs[ORDER[p]]
                    total = a[zz, core, q].astype(F32) + r[zz, q].astype(F32)
                    if d:
                        sx[d, p] = total.astype(BF16)
                    else:
                        acc[p] = total
                if d:
                    part = pl.ds(4 * half, 4)
                    m = remote(sx.at[d, part], qx.at[x, part], x_send.at[i, d, half], x_recv.at[i, x, half], (lat, q * 2 + yl))
                    m.start()
                    sends.append(m)
    def along_z(i, sx, qx, acc, tz, zb):
        for half in range(2):
            part = pl.ds(4 * half, 4)
            for d in (1, 3, 2):
                q = xq[d]
                remote(sx.at[d, part], qx.at[q, part], x_send.at[i, d, half], x_recv.at[i, q, half], (lat, q * 2 + yl)).wait_recv()
            for p in range(4 * half, 4 * half + 4):
                d = ORDER[p]
                total = acc[p] + (qx[xq[1], p].astype(F32) + qx[xq[3], p].astype(F32)) + qx[xq[2], p].astype(F32)
                if d:
                    tz[d] = total.astype(BF16)
                    m = remote(tz.at[d], zb.at[z], z_send.at[i, d], z_recv.at[i, z], (lat_of(yh, zs[d]), lon))
                    m.start()
                    sends.append(m)
                else:
                    acc[p] = total
    ys = [(1 - yh, yl, (across, lon)), (yh, 1 - yl, (lat, beside)), (1 - yh, 1 - yl, (across, beside))]
    def along_y(i, acc, tz, zb, u, f, l):
        size = S1 if i == 2 else S2
        total = acc[7]
        for d in near:
            zz = zs[d]
            remote(tz.at[d], zb.at[zz], z_send.at[i, d], z_recv.at[i, zz], (lat_of(yh, zz), lon)).wait_recv()
            total = total + zb[zz].astype(F32)
        u[...] = total
        def cut(shift):
            for y in range(2):
                for piece, lane, row, at, length in flat_moves(size, shift, ROWS[i], y):
                    f[2 * y + piece, :, lane : lane + length] = u[row : row + 1, at : at + length]
        if i == 2:
            cut(0)
        else:
            @pl.when(lax.rem(x, 2) == 0)
            def _():
                cut(0)
            @pl.when(lax.rem(x, 2) == 1)
            def _():
                cut(96)
        me = 2 * yh + yl
        for d, (h, b, peer) in enumerate(ys):
            m = remote(f.at[2 * h + b], l.at[me], y_send.at[i, d], y_recv.at[i, me], peer)
            m.start()
            sends.append(m)
        l[me] = f[me]
    def total_of(i, f, l):
        for d, (h, b, peer) in enumerate(ys):
            remote(f.at[2 * h + b], l.at[2 * h + b], y_send.at[i, d], y_recv.at[i, 2 * h + b], peer).wait_recv()
        return (((l[0] + l[1]) + (l[2] + l[3])) * (1.0 / LOSS_CELLS)).reshape(S1 if i == 2 else S2)

    dt[...] = ds3[1, 2:34, 0:32, :].reshape(1024, 192).T
    wgrad(hs2, 2, g3)
    c3 = to_partner(0, g3, a3, r3)

    def d_two(s):
        n = 12
        v = tconv(ds3, k3, s, n)
        _, dv = deriv(p2[pl.ds(s + 2, n)])
        put_shifted(ds2, s, n, jnp.where(rows_ok(s, n, -1), v * dv, 0.0))
    chunks(35, 12, d_two)
    along_x(0, c3, a3, r3, s3, q3, acc3)
    dt[...] = ds2[1, 1:33, 0:32, :].reshape(1024, 192).T
    wgrad(hs1, 3, g2)
    c2 = to_partner(1, g2, a2, r2)

    def b_one(s):
        n = 11
        v = jnp.where(rows_ok(s, n, 0), tconv(ds2, k2, s, n), 0.0)
        bs[1, pl.ds(s, n)] = v.astype(BF16)
        bs[2, pl.ds(s, n)] = pltpu.roll(v, W - 1, 1).astype(BF16)
    chunks(33, 11, b_one, 0, 1)
    along_x(1, c2, a2, r2, s2, q2, acc2)
    chunks(33, 11, b_one, 1, 2)
    along_z(0, s3, q3, acc3, t3, z3)
    chunks(33, 11, b_one, 2, 3)
    dt[...] = bs[1, 0:32, 0:32, :].reshape(1024, 192).T
    for a in range(3):
        src = x1 if a == 1 else x0
        off = 4 + (a == 2)
        win = src[off : off + 32, 0:32, :].reshape(1024, 384)
        g1[384 * a : 384 * a + 384, :] = mm(dt[...], win).T
    c1 = to_partner(2, g1, a1, r1)
    along_z(1, s2, q2, acc2, t2, z2)
    def k1t(a, b):
        n0 = (3 * a + b) * 128
        return k1[n0 : n0 + 128]
    def gin(i):
        n = 8
        here = bs[1, pl.ds(i, n), 0:32, :].reshape(n * 32, 192)
        right = bs[2, pl.ds(i, n), 0:32, :].reshape(n * 32, 192)
        below = bs[1, pl.ds(i + 1, n), 0:32, :].reshape(n * 32, 192)
        corner = bs[2, pl.ds(i + 1, n), 0:32, :].reshape(n * 32, 192)
        ee = mmt(here, k1t(1, 1))
        eo = mmt(right, k1t(1, 0)) + mmt(here, k1t(1, 2))
        oe = mmt(below, k1t(0, 1)) + mmt(here, k1t(2, 1))
        oo = mmt(corner, k1t(0, 0)) + mmt(below, k1t(0, 2)) + mmt(right, k1t(2, 0)) + mmt(here, k1t(2, 2))
        il[pl.ds(0, n * 32, stride=2), :] = ee
        il[pl.ds(1, n * 32, stride=2), :] = eo
        il[pl.ds(n * 64, n * 32, stride=2), :] = oe
        il[pl.ds(n * 64 + 1, n * 32, stride=2), :] = oo
        even = il[0 : n * 64, :].reshape(n, 64, 128).astype(BF16)
        odd = il[n * 64 : n * 128, :].reshape(n, 64, 128).astype(BF16)
        for m in range(n):
            gin_ref[2 * (i + m)] = even[m]
            gin_ref[2 * (i + m) + 1] = odd[m]
    chunks(32, 8, gin, 0, 1)
    along_x(2, c1, a1, r1, s1, q1, acc1)
    chunks(32, 8, gin, 1, 4)
    along_z(2, s1, q1, acc1, t1, z1)
    along_y(0, acc3, t3, z3, u3, f3, l3)
    along_y(1, acc2, t2, z2, u2, f2, l2)
    o3[...] = total_of(0, f3, l3)
    o2[...] = total_of(1, f2, l2)
    along_y(2, acc1, t1, z1, u1, f1, l1)
    o1[...] = total_of(2, f1, l1)
    for k in sends:
        k.wait_send()


def level(w1, w2, w3, x, c):
    V, D = pltpu.VMEM, pltpu.SemaphoreType.DMA
    vm = pl.BlockSpec(memory_space=pltpu.VMEM)
    hbm = pl.BlockSpec(memory_space=pl.ANY)
    sds = jax.ShapeDtypeStruct
    def each(shape_of, dtype=BF16):
        return [V(shape_of(r), dtype) for r in PACKED]
    def flats():
        return [V((4, 1, n), F32) for n in (S2, S2, S1)]
    halos = [(10, 64, 128)] * 4 + [(10, 16, 128)] * 4 + [(32, 8, 192)] * 2 + [(3, 32, 192)] * 2 + [(3, 8, 192)] * 4
    return pl.pallas_call(
        level_kernel,
        out_shape=(sds((32, 32, 192), BF16), sds((64, 64, 128), BF16), sds((S1,), F32), sds((S2,), F32), sds((S2,), F32)),
        in_specs=[vm, vm, vm, hbm, hbm],
        out_specs=(vm,) * 5,
        scratch_shapes=[
            V((64, 64, 128), BF16), V((32, 32, 192), BF16), V((1, 3456), F32), V((LON, 1, 3456), F32), V((72, 384), F32),
            V((XS, 56, 128), BF16), V((2, 10, 64, 128), BF16), *[V(s, BF16) for s in halos],
            V((GROUPS, XS, 56, 128), BF16), V((224, 128), F32),
            V((90 * PITCH, 128), F32), V((42, W, 384), BF16), V((42, W, 384), BF16),
            V((1728, 192), F32), V((1728, 192), F32), V((1152, 192), F32),
            V((1152, 192), BF16), V((1728, 192), BF16), V((1728, 192), BF16),
            V((37, W, 192), F32), V((3, 41, W, 192), BF16), V((3, 39, W, 192), BF16),
            V((3, 37, W, 192), BF16), V((3, 35, W, 192), BF16), V((3, 37, W, 192), BF16),
            V((39, W, 192), F32), V((192, 1024), BF16), V((1152, 192), F32), V((1728, 192), F32), V((1728, 192), F32),
            V((48, 128), F32), V((1024, 128), F32),
            *each(lambda r: (ZS, 2, XS, r, 128)), *each(lambda r: (ZS, XS, r, 128)),
            *each(lambda r: (XS, ZS, r, 128)), *each(lambda r: (XS, ZS, r, 128)),
            *each(lambda r: (ZS, r, 128), F32), *each(lambda r: (ZS, r, 128)), *each(lambda r: (ZS, r, 128)),
            *each(lambda r: (r, 128), F32), *flats(), *flats(),
            D((2,)), D((LON,)), D((LON,)), D((20,)), D((20,)), D((16,)), D((GROUPS, XS)), D((16, XS)), D((16,)), D((GROUPS,)),
            D((3,)), D((3,)), D((3, XS, 2)), D((3, XS, 2)), D((3, ZS)), D((3, ZS)), D((3, 4)), D((3, 4)),
        ],
        compiler_params=pltpu.CompilerParams(collective_id=0, has_side_effects=True, vmem_limit_bytes=63 * 1024 * 1024),
        name="level",
    )(w1, w2, w3, x, c)


def finish_kernel(f, g, a, b, c, fo, go, ao, bo, co, fv, gv, av, bv, cv, isem, osem):
    trips = [(f, fv, fo), (a, av, ao), (b, bv, bo), (c, cv, co)]
    trips += [(g.at[16 * k : 16 * k + 16], gv.at[16 * k : 16 * k + 16], go.at[16 * k : 16 * k + 16]) for k in range(4)]
    ins = [pltpu.make_async_copy(src, mid, isem.at[i]) for i, (src, mid, _) in enumerate(trips)]
    outs = [pltpu.make_async_copy(mid, dst, osem.at[i]) for i, (_, mid, dst) in enumerate(trips)]
    for k in ins:
        k.start()
    for k, m in zip(ins, outs):
        k.wait()
        m.start()
    for m in outs:
        m.wait()


def finish(*arrays):
    hbm = pl.BlockSpec(memory_space=pl.ANY)
    return pl.pallas_call(
        finish_kernel,
        out_shape=tuple(jax.ShapeDtypeStruct(a.shape, a.dtype) for a in arrays),
        in_specs=[hbm] * 5,
        out_specs=(hbm,) * 5,
        scratch_shapes=[*[pltpu.VMEM(a.shape, a.dtype) for a in arrays],
                        pltpu.SemaphoreType.DMA((8,)), pltpu.SemaphoreType.DMA((8,))],
        name="results",
    )(*arrays)


def local(inputs, w_first, w_second, w_third, cotangent):
    return finish(*level(w_first, w_second, w_third, inputs, cotangent))


def solution(mesh):
    tile, flat = P("lat", "lon", None), P(("lat", "lon"))
    return jax.shard_map(
        local,
        mesh=mesh,
        in_specs=(tile, flat, flat, flat, tile),
        out_specs=(tile, tile, flat, flat, flat),
        check_vma=False,
    )
```
